32 devices in a mesh: date: 8 (over y, x, core), bucket: 4 (over z).
Axes of the slice: x: 2, y: 2, z: 4, core: 2. Of those that a mesh axis runs over, the one named last changes fastest.
Arguments:
- transition: bfloat16 [32, 8, 512, 512], P('date', 'bucket'), may hold values from -1 to 1, as said below
- shocks: bfloat16 [32, 8, 512, 16, 128], P('date', 'bucket'), may hold values from -1.5 to 1.5
- step_days: int32 [32], P('date'), may hold values from 7 to 31
- readout: bfloat16 [8, 64, 512], P('bucket'), may hold values from -0.25 to 0.25
- risk_weight: float32 [8, 64], P('bucket'), may hold values from 0.05 to 0.5
- correlation: float32 [8, 64, 64], P('bucket'), may hold values from -1 to 1, as said below
- cross_gamma: float32 [8, 8], replicated, may hold values from 0.1 to 0.3
- discount: float32 [32, 16, 128], P('date', 'bucket'), may hold values from 0.1 to 1
- path_counts: int32 [16], replicated, may hold values from 64 to 128
Outputs:
- margin: float32 [32, 16, 128], P('date', 'bucket')
- adjustment: float32 [], replicated
The draws below stay inside these ranges and needn't reach their ends.
Inputs may be any that keep to these rules, and one draw needn't show every extreme that they name: Each matrix transition[t, b] has entries of magnitude at most one. Each correlation[b] is symmetric positive definite with unit diagonal.
All inputs are finite; a program needn't handle non-finite values.
Results may differ from the reference program's by a relative error of at most 0.013.
Values may be sent and summed in bfloat16 or wider, within the bound.
No kernel may reach another device: no remote copies, remote signals or barrier semaphores. Data moves between devices by JAX's collectives and lax.ppermute only.
A program may use at most 64 MiB of HBM per device.

```python
import math
import jax
import jax.numpy as jnp
from jax import lax

FEAT = 512
SENSB = 64
RISK_BUCKETS = 8
MICRO = 16
P_MB = 128
EVOLVE_DATES = 32


def draw_transition(key, part):
    key_rate = jax.random.fold_in(key, 11)
    section_key = jax.random.fold_in(key, 12)
    key_noise = jax.random.fold_in(key, 13)
    lowest = 0.5 / EVOLVE_DATES
    highest = 10.0 / EVOLVE_DATES
    rates = jnp.exp(jax.random.uniform(key_rate, (RISK_BUCKETS, FEAT), jnp.float32, math.log(lowest), math.log(highest)))
    dates_per_section = jax.random.randint(section_key, (RISK_BUCKETS, 3), 0, EVOLVE_DATES)
    bucket_matches = jnp.any(dates_per_section[None, :, :] == jnp.arange(EVOLVE_DATES)[:, None, None], axis=-1)
    factor = jnp.where(bucket_matches, 0.7, 1.0).astype(jnp.float32)
    retained = jnp.exp(-rates)[None, :, :] * factor[:, :, None]
    noise = jax.random.normal(key_noise, (EVOLVE_DATES, RISK_BUCKETS, FEAT, FEAT), jnp.float32) * (0.2 / math.sqrt(FEAT))
    skewed = (noise - jnp.swapaxes(noise, 2, 3)) / math.sqrt(2.0)
    matrix = retained[:, :, :, None] * (jnp.eye(FEAT, dtype=jnp.float32)[None, None] + skewed)
    return matrix.astype(jnp.bfloat16)


def draw_correlation(key, part):
    key_noise = jax.random.fold_in(key, 21)
    key_common = jax.random.fold_in(key, 22)
    noise = jax.random.normal(key_noise, (RISK_BUCKETS, SENSB, SENSB), jnp.float32)
    factor = jnp.eye(SENSB, dtype=jnp.float32)[None] + 0.4 * noise / math.sqrt(SENSB)
    product = jnp.einsum('bij,bkj->bik', factor, factor, precision=lax.Precision.HIGHEST)
    diagonal_terms = jnp.sqrt(jnp.diagonal(product, axis1=1, axis2=2))
    normalized = product / (diagonal_terms[:, :, None] * diagonal_terms[:, None, :])
    common = jax.random.uniform(key_common, (RISK_BUCKETS,), jnp.float32, 0.2, 0.5)
    blended = (1.0 - common)[:, None, None] * normalized + common[:, None, None]
    return blended.astype(jnp.float32)


def set_ends(drawn, own_key, least, high):
    longest = drawn.shape.index(max(drawn.shape))
    spots = []
    for shift in (0, 1):
        where = [jax.random.randint(jax.random.fold_in(own_key, axis), (), 0, length) for axis, length in enumerate(drawn.shape)]
        where[longest] = (where[longest] + shift) % drawn.shape[longest]
        spots.append(tuple(where))
    return drawn.at[spots[0]].set(least).at[spots[1]].set(high)


def level_of(own_key, extent, cuts, low, top_value):
    def one(dim, parts):
        heights = jax.random.uniform(jax.random.fold_in(jax.random.fold_in(own_key, 6), dim), (parts,), jnp.float32, low / len(cuts), top_value / len(cuts))
        return jnp.repeat(jnp.exp(heights), extent[dim] // parts).reshape((-1,) + (1,) * (len(extent) - dim - 1))

    level = one(*cuts[0])
    for cut in cuts[1:]:
        level = level * one(*cut)
    return level


def scatter_about(key, extent, deviation, limit, pieces=(), kind=jnp.bfloat16):
    array = deviation * jax.random.normal(key, extent, jnp.float32)
    if pieces:
        array = array * level_of(key, extent, pieces, -0.22, 0.18)
    return jnp.clip(array, -limit, limit).astype(kind)


def setup_inputs(seed: int = 0) -> dict:
    key_list = jax.random.split(jax.random.key(seed), 10)
    transition = draw_transition(jax.random.fold_in(key_list[9], 71), 0)
    shocks = scatter_about(key_list[1], (EVOLVE_DATES, RISK_BUCKETS, FEAT, MICRO, P_MB), 0.25, 1.5, ((0, 8), (1, 4)))
    step_days = set_ends(jax.random.randint(key_list[2], (EVOLVE_DATES,), 7, 32), jax.random.fold_in(key_list[2], 1), 7, 31).astype(jnp.int32)
    readout = scatter_about(key_list[3], (RISK_BUCKETS, SENSB, FEAT), FEAT ** -0.5, 0.25, ((0, 4),))
    risk_weight = jnp.clip(jnp.exp(math.log(0.5) - 2.3025851 * jax.random.uniform(key_list[4], (RISK_BUCKETS, SENSB), jnp.float32) ** level_of(key_list[4], (RISK_BUCKETS, SENSB), ((0, 4),), -0.2, 0.2)), 0.05, 0.5)
    correlation = draw_correlation(jax.random.fold_in(key_list[9], 71), 0)
    cross_gamma = jnp.clip(jax.random.uniform(key_list[6], (RISK_BUCKETS, RISK_BUCKETS), jnp.float32, 0.1, 0.3), 0.1, 0.3)
    discount = jnp.clip(jnp.exp(math.log(1.0) - 2.3025851 * jax.random.uniform(key_list[7], (EVOLVE_DATES, MICRO, P_MB), jnp.float32) ** level_of(key_list[7], (EVOLVE_DATES, MICRO, P_MB), ((0, 8), (1, 4)), -0.2, 0.2)), 0.1, 1.0)
    path_counts = set_ends(jax.random.randint(key_list[8], (MICRO,), P_MB // 2, P_MB + 1), jax.random.fold_in(key_list[8], 1), P_MB // 2, P_MB).astype(jnp.int32)
    return dict(transition=transition, shocks=shocks, step_days=step_days, readout=readout, risk_weight=risk_weight, correlation=correlation, cross_gamma=cross_gamma, discount=discount, path_counts=path_counts)


epsilon = 1e-06

def reference(transition, shocks, step_days, readout, risk_weight, correlation, cross_gamma, discount, path_counts):
    path_total = MICRO * P_MB
    flat_shocks = shocks.reshape(EVOLVE_DATES, RISK_BUCKETS, FEAT, path_total)
    scales = jnp.sqrt(step_days.astype(jnp.float32) / 30.0)

    def advance_date(carried, inputs):
        matrix, shock_slice, date_scale = inputs
        propagated = jnp.einsum('bij,bjp->bip', matrix.astype(jnp.float32), carried.astype(jnp.float32), precision=lax.Precision.HIGHEST)
        carried = (propagated + date_scale * shock_slice.astype(jnp.float32)).astype(jnp.bfloat16)
        sensitivity = jnp.einsum('bsf,bfp->bsp', readout.astype(jnp.float32), carried.astype(jnp.float32), precision=lax.Precision.HIGHEST)
        weighted = risk_weight[:, :, None] * sensitivity
        correlated = jnp.einsum('bst,btp->bsp', correlation, weighted, precision=lax.Precision.HIGHEST)
        within_sq = lax.optimization_barrier(jnp.sum(weighted * correlated, axis=1)) + epsilon
        within_root = jnp.sqrt(within_sq)
        net_sum = jnp.clip(lax.optimization_barrier(jnp.sum(weighted, axis=1)), -within_root, within_root)
        return (carried, (within_sq, net_sum))
    initial = jnp.zeros((RISK_BUCKETS, FEAT, path_total), jnp.bfloat16)
    final_state, outputs = lax.scan(advance_date, initial, (transition, flat_shocks, scales))
    within_all, net_all = outputs
    gamma_off = 0.5 * (cross_gamma + cross_gamma.T) * (1.0 - jnp.eye(RISK_BUCKETS, dtype=jnp.float32))
    coupled = jnp.einsum('bc,dcp->dbp', gamma_off, net_all, precision=lax.Precision.HIGHEST)
    squares = lax.optimization_barrier(jnp.sum(within_all + net_all * coupled, axis=1)).reshape(EVOLVE_DATES, MICRO, P_MB)
    alive_mask = jnp.arange(P_MB, dtype=jnp.int32)[None, :] < path_counts[:, None]
    margin = jnp.where(alive_mask[None], jnp.sqrt(squares), jnp.float32(0.0))
    weights = step_days.astype(jnp.float32) / 365.0
    adjustment = jnp.sum(weights[:, None, None] * discount * margin / path_counts.astype(jnp.float32)[None, :, None])
    return (margin, adjustment)
```

```python
import functools

import jax
import jax.numpy as jnp
from jax import lax
from jax.experimental import pallas as pl
from jax.experimental.pallas import tpu as pltpu
from jax.sharding import PartitionSpec as P

epsilon = 1e-06
f32 = jnp.float32
bf16 = jnp.bfloat16


def dot(a, b):
    return jnp.dot(a, b, preferred_element_type=f32)


def split(x):
    high = x.astype(bf16)
    return high, (x - high.astype(f32)).astype(bf16)


def operator_kernel(dates, a_ref, r_ref, w_ref):
    features = a_ref.shape[-1]
    sens = r_ref.shape[1]
    product = a_ref[0, 0]
    for t in range(dates):
        if t:
            product = dot(a_ref[t, 0], product).astype(bf16)
        row = features + t * sens
        w_ref[0, row : row + sens, :] = dot(r_ref[0], product).astype(bf16)
    w_ref[0, :features, :] = product


def local_kernel(dates, scale_ref, x_ref, a_ref, r_ref, e_ref, s_ref, rows_ref, state_ref):
    features, micro, lanes = x_ref.shape[2:]
    sens = r_ref.shape[1]
    pair = 2
    for t in range(dates):
        rows_ref[...] = x_ref[t, 0].astype(f32).reshape(features * micro, lanes)
        scale = scale_ref[t]
        for m in range(0, micro, pair):
            cols = slice(m * lanes, (m + pair) * lanes)
            shock = jnp.concatenate(
                [rows_ref[pl.ds(m + i, features, stride=micro), :] for i in range(pair)], axis=1
            )
            total = scale * shock
            if t:
                total = total + dot(a_ref[t, 0], state_ref[(t - 1) % 2, :, cols])
            state = total.astype(bf16)
            state_ref[t % 2, :, cols] = state
            seen = dot(r_ref[0], state)
            for i in range(pair):
                part = slice(i * lanes, (i + 1) * lanes)
                s_ref[m + i, 0, t * sens : (t + 1) * sens, :] = seen[:, part]
                if t == dates - 1:
                    e_ref[m + i, 0] = state[:, part]


def tick_kernel(dates, at_ref, in_ref, w_ref, e_ref, s_ref, rw_ref, c_ref, out_ref, stat_ref):
    features = in_ref.shape[1]
    lanes = in_ref.shape[2]
    sens = rw_ref.shape[1]
    bucket = pl.program_id(0)
    buckets = pl.num_programs(0)
    moved = dot(w_ref[0], in_ref[0])
    out_ref[0] = (moved[:features] + e_ref[0, 0].astype(f32)).astype(bf16)
    seen = moved[features:] + s_ref[0, 0]
    ws = jnp.concatenate(
        [rw_ref[0] * seen[t * sens : (t + 1) * sens] for t in range(dates)], axis=1
    )
    c_high, c_low = split(c_ref[0])
    w_high, w_low = split(ws)
    mixed = dot(
        jnp.concatenate([c_high, c_low, c_high], axis=1),
        jnp.concatenate([w_high, w_high, w_low], axis=0),
    )
    within = jnp.sum(ws * mixed, axis=0, keepdims=True) + epsilon
    root = jnp.sqrt(within)
    net = jnp.clip(jnp.sum(ws, axis=0, keepdims=True), -root, root)

    @pl.when(bucket == 0)
    def _():
        stat_ref[0:1, :] = within

    @pl.when(bucket > 0)
    def _():
        stat_ref[0:1, :] += within

    stat_ref[pl.ds(bucket + 1, 1), :] = net


def shards(
    transition,
    shocks,
    step_days,
    readout,
    risk_weight,
    correlation,
    cross_gamma,
    discount,
    path_counts,
):
    position = lax.axis_index("date")
    segments = lax.axis_size("date")
    zs = lax.axis_size("bucket")
    z = lax.axis_index("bucket")
    dates, buckets, features, batches, lanes = shocks.shape
    sens = readout.shape[1]
    scales = jnp.sqrt(step_days.astype(f32) / 30.0)
    group = batches // 2
    rows = features + dates * sens

    ends, seen = pl.pallas_call(
        functools.partial(local_kernel, dates),
        out_shape=(
            jax.ShapeDtypeStruct((batches, buckets, features, lanes), bf16),
            jax.ShapeDtypeStruct((batches, buckets, dates * sens, lanes), f32),
        ),
        grid=(buckets, 2),
        in_specs=[
            pl.BlockSpec(memory_space=pltpu.SMEM),
            pl.BlockSpec((dates, 1, features, group, lanes), lambda b, g: (0, b, 0, g, 0)),
            pl.BlockSpec((dates, 1, features, features), lambda b, g: (0, b, 0, 0)),
            pl.BlockSpec((1, sens, features), lambda b, g: (b, 0, 0)),
        ],
        out_specs=(
            pl.BlockSpec((group, 1, features, lanes), lambda b, g: (g, b, 0, 0)),
            pl.BlockSpec((group, 1, dates * sens, lanes), lambda b, g: (g, b, 0, 0)),
        ),
        scratch_shapes=[
            pltpu.VMEM((features * group, lanes), f32),
            pltpu.VMEM((2, features, group * lanes), bf16),
        ],
        name="local",
    )(scales, shocks, transition, readout)

    operators = pl.pallas_call(
        functools.partial(operator_kernel, dates),
        out_shape=jax.ShapeDtypeStruct((buckets, rows, features), bf16),
        grid=(buckets,),
        in_specs=[
            pl.BlockSpec((dates, 1, features, features), lambda b: (0, b, 0, 0)),
            pl.BlockSpec((1, sens, features), lambda b: (b, 0, 0)),
        ],
        out_specs=pl.BlockSpec((1, rows, features), lambda b: (b, 0, 0)),
        name="operators",
    )(transition, readout)

    weight_column = risk_weight[:, :, None]
    tick = pl.pallas_call(
        functools.partial(tick_kernel, dates),
        out_shape=(
            jax.ShapeDtypeStruct((buckets, features, lanes), bf16),
            jax.ShapeDtypeStruct((buckets + 1, dates * lanes), f32),
        ),
        grid_spec=pltpu.PrefetchScalarGridSpec(
            num_scalar_prefetch=1,
            grid=(buckets,),
            in_specs=[
                pl.BlockSpec((1, features, lanes), lambda b, c: (b, 0, 0)),
                pl.BlockSpec((1, rows, features), lambda b, c: (b, 0, 0)),
                pl.BlockSpec((1, 1, features, lanes), lambda b, c: (c[0], b, 0, 0)),
                pl.BlockSpec((1, 1, dates * sens, lanes), lambda b, c: (c[0], b, 0, 0)),
                pl.BlockSpec((1, sens, 1), lambda b, c: (b, 0, 0)),
                pl.BlockSpec((1, sens, sens), lambda b, c: (b, 0, 0)),
            ],
            out_specs=(
                pl.BlockSpec((1, features, lanes), lambda b, c: (b, 0, 0)),
                pl.BlockSpec((buckets + 1, dates * lanes), lambda b, c: (0, 0)),
            ),
        ),
        cost_estimate=pl.CostEstimate(
            flops=2 * buckets * rows * features * lanes, bytes_accessed=2**22, transcendentals=0
        ),
        name="tick",
    )

    skew = 2
    ticks = batches + skew * (segments - 1)
    forward = [(i, i + 1) for i in range(segments - 1)]
    received = [jnp.zeros((buckets, features, lanes), bf16)] * skew
    stats = []
    for step in range(ticks):
        at = jnp.clip(step - skew * position, 0, batches - 1).astype(jnp.int32).reshape(1)
        leaving, stat = tick(
            at, received[step], operators, ends, seen, weight_column, correlation
        )
        stats.append(stat)
        if step < ticks - skew:
            received.append(lax.ppermute(leaving, "date", forward))
    stats = jnp.stack(stats)
    mine = lax.dynamic_slice_in_dim(stats, skew * position, batches, 0)

    message = jnp.concatenate(
        [mine.reshape(-1, lanes), discount.reshape(-1, lanes)], axis=0
    )
    gathered = [message]
    for k in range(1, zs):
        gathered.append(
            lax.ppermute(message, "bucket", [(i, (i + k) % zs) for i in range(zs)])
        )
    gathered = jnp.roll(jnp.stack(gathered[::-1]), z + 1, axis=0)
    count_rows = mine.size // lanes
    parts = gathered[:, :count_rows].reshape(zs, batches, buckets + 1, dates, lanes)
    local_micro = discount.shape[1]
    discounts = gathered[:, count_rows:].reshape(zs, dates, local_micro, lanes)
    discounts = jnp.swapaxes(discounts, 0, 1).reshape(dates, batches, lanes)
    within = jnp.sum(parts[:, :, 0], axis=0)
    nets = jnp.swapaxes(parts[:, :, 1:], 1, 2).reshape(zs * buckets, batches, dates, lanes)
    gamma = (
        0.5
        * (cross_gamma + cross_gamma.T)
        * (1.0 - jnp.eye(cross_gamma.shape[0], dtype=f32))
    )
    coupled = jnp.sum(gamma[:, :, None, None, None] * nets[None], axis=1)
    squares = within + jnp.sum(nets * coupled, axis=0)
    squares = jnp.swapaxes(squares, 0, 1)
    alive = jnp.arange(lanes, dtype=jnp.int32)[None, :] < path_counts[:, None]
    margins = jnp.where(alive[None], jnp.sqrt(squares), f32(0.0))
    weights = step_days.astype(f32) / 365.0
    total = jnp.sum(
        weights[:, None, None] * discounts * margins / path_counts.astype(f32)[None, :, None]
    )
    total = jnp.full((8, lanes), total)
    step = 1
    while step < segments:
        total = total + lax.ppermute(
            total, "date", [(i, i ^ step) for i in range(segments)]
        )
        step *= 2
    margin = lax.dynamic_slice_in_dim(margins, z * local_micro, local_micro, 1)
    return (margin, total[0, 0])


def solution(mesh):
    in_specs = (
        P("date", "bucket", None, None),
        P("date", "bucket", None, None, None),
        P("date"),
        P("bucket", None, None),
        P("bucket", None),
        P("bucket", None, None),
        P(),
        P("date", "bucket", None),
        P(),
    )
    out_specs = (P("date", "bucket", None), P())
    return jax.shard_map(shards, mesh=mesh, in_specs=in_specs, out_specs=out_specs, check_vma=False)
```

```python
import functools

import jax
import jax.numpy as jnp
from jax import lax
from jax.experimental import pallas as pl
from jax.experimental.pallas import tpu as pltpu
from jax.sharding import PartitionSpec as P

epsilon = 1e-06
f32 = jnp.float32
bf16 = jnp.bfloat16
pair = 2
flight = 3


def dot(a, b):
    return jnp.dot(a, b, preferred_element_type=f32)


def split(x):
    high = x.astype(bf16)
    return high, (x - high.astype(f32)).astype(bf16)


def cost(flops, read):
    return pl.CostEstimate(flops=flops, bytes_accessed=read, transcendentals=0)


def operator_kernel(dates, a_ref, r_ref, w_ref):
    features = a_ref.shape[-1]
    sens = r_ref.shape[1]
    product = a_ref[0, 0]
    for t in range(dates):
        if t:
            product = dot(a_ref[t, 0], product).astype(bf16)
        row = features + t * sens
        w_ref[0, row : row + sens, :] = dot(r_ref[0], product).astype(bf16)
    w_ref[0, :features, :] = product


def local_kernel(scale_ref, octet_ref, x_ref, a_ref, r_ref, out_ref, rows_ref, state_ref):
    features, micro, lanes = x_ref.shape[2:]
    sens = r_ref.shape[1]
    t = pl.program_id(1)
    rows_ref[...] = x_ref[0, 0].astype(f32).reshape(features * micro, lanes)
    scale = scale_ref[t]
    width = pair * lanes

    def shock(q):
        return scale * jnp.concatenate(
            [rows_ref[pl.ds(q * pair + i, features, stride=micro), :] for i in range(pair)],
            axis=1,
        )

    @pl.when(t == 0)
    def _():
        for q in range(micro // pair):
            state_ref[:, q * width : (q + 1) * width] = shock(q).astype(bf16)

    @pl.when(t > 0)
    def _():
        for q in range(micro // pair):
            cols = slice(q * width, (q + 1) * width)
            state_ref[:, cols] = (shock(q) + dot(a_ref[0, 0], state_ref[:, cols])).astype(bf16)

    row = pl.multiple_of(features + t * sens, sens)
    for q in range(micro // pair):
        state = state_ref[:, q * width : (q + 1) * width]
        out_ref[0, q, pl.ds(row, sens), :] = dot(r_ref[0], state).astype(bf16)

    @pl.when(t == pl.num_programs(1) - 1)
    def _():
        for q in range(micro // pair):
            out_ref[0, q, :features, :] = state_ref[:, q * width : (q + 1) * width]


def join_operator_kernel(core_ref, mine_ref, other_ref, p_ref, q_ref, late_ref):
    features = mine_ref.shape[2]
    first = core_ref[0] == 0
    mine, other = mine_ref[0], other_ref[0]
    early = jnp.where(first, mine, other)
    late = jnp.where(first, other, mine)
    joined = dot(late, early[:features]).astype(bf16)
    p_ref[0] = joined[:features]
    seen = late.shape[0] - features
    q_ref[0, :seen, :] = early[features:]
    q_ref[0, seen:, :] = joined[features:]
    late_ref[0] = late


def join_state_kernel(core_ref, mine_ref, other_ref, late_ref, seen_ref, *end_refs):
    features = late_ref.shape[2]
    first = core_ref[0] == 0
    mine, other = mine_ref[0, 0], other_ref[0, 0]
    early = jnp.where(first, mine, other)
    late = jnp.where(first, other, mine)
    joined = dot(late_ref[0], early[:features]) + late.astype(f32)
    seen = late.shape[0] - features
    seen_ref[0, :seen, :] = early[features:].astype(f32)
    seen_ref[0, seen:, :] = joined[features:]
    end = joined[:features].astype(bf16)
    for q, end_ref in enumerate(end_refs):

        @pl.when(pl.program_id(0) == q)
        def _():
            end_ref[...] = end


def stage_kernel(up_ref, mine_ref, other_ref, a_ref, out_ref):
    up = up_ref[0] == 1
    mine, other = mine_ref[...], other_ref[...]
    early = jnp.where(up, other, mine)
    late = jnp.where(up, mine, other)
    out_ref[...] = (dot(a_ref[0], early) + late.astype(f32)).astype(bf16)


def final_kernel(dates, up_ref, first_ref, last_ref, phi_ref, q_ref, seen_ref, rw_ref, c_ref, out_ref):
    sens = rw_ref.shape[1]
    width = first_ref.shape[1]
    first = first_ref[...].astype(f32)
    first = jnp.where(up_ref[0] == 1, first, jnp.zeros_like(first))
    entering = (first + dot(phi_ref[0], last_ref[...])).astype(bf16)
    seen = seen_ref[0] + dot(q_ref[0], entering)
    weight = rw_ref[0]
    ws = jnp.concatenate(
        [weight * seen[t * sens : (t + 1) * sens] for t in range(dates)], axis=1
    )
    c_high, c_low = split(c_ref[0])
    w_high, w_low = split(ws)
    mixed = dot(
        jnp.concatenate([c_high, c_low, c_high], axis=1),
        jnp.concatenate([w_high, w_high, w_low], axis=0),
    )
    within = jnp.sum(ws * mixed, axis=0, keepdims=True) + epsilon
    root = jnp.sqrt(within)
    net = jnp.clip(jnp.sum(ws, axis=0, keepdims=True), -root, root)
    for t in range(dates):
        out_ref[0, t : t + 1, :] = within[:, t * width : (t + 1) * width]
        out_ref[1, t : t + 1, :] = net[:, t * width : (t + 1) * width]


def shards(
    transition,
    shocks,
    step_days,
    readout,
    risk_weight,
    correlation,
    cross_gamma,
    discount,
    path_counts,
):
    position = lax.axis_index("date")
    segments = lax.axis_size("date")
    zs = lax.axis_size("bucket")
    z = lax.axis_index("bucket")
    dates, buckets, features, batches, lanes = shocks.shape
    sens = readout.shape[1]
    scales = jnp.sqrt(step_days.astype(f32) / 30.0)
    half = batches // 2
    pieces = half // pair
    width = pair * lanes
    seen_rows = dates * sens
    rows = features + seen_rows
    core = lax.rem(position, 2)
    core_flag = core.astype(jnp.int32).reshape(1)
    stages = (segments // 2).bit_length() - 1
    ups = [lax.rem(position // (2 << s), 2).astype(jnp.int32).reshape(1) for s in range(stages)]
    swap = [(i, i ^ 1) for i in range(segments)]
    smem = pl.BlockSpec(memory_space=pltpu.SMEM)

    operators = pl.pallas_call(
        functools.partial(operator_kernel, dates),
        out_shape=jax.ShapeDtypeStruct((buckets, rows, features), bf16),
        grid=(buckets,),
        in_specs=[
            pl.BlockSpec((dates, 1, features, features), lambda b: (0, b, 0, 0)),
            pl.BlockSpec((1, sens, features), lambda b: (b, 0, 0)),
        ],
        out_specs=pl.BlockSpec((1, rows, features), lambda b: (b, 0, 0)),
        cost_estimate=cost(2 * buckets * dates * features**3, 2**23),
        name="operators",
    )(transition, readout)

    def local(octet):
        return pl.pallas_call(
            local_kernel,
            out_shape=jax.ShapeDtypeStruct((buckets, pieces, rows, width), bf16),
            grid_spec=pltpu.PrefetchScalarGridSpec(
                num_scalar_prefetch=2,
                grid=(buckets, dates),
                in_specs=[
                    pl.BlockSpec(
                        (1, 1, features, half, lanes), lambda b, t, s, o: (t, b, 0, o[0], 0)
                    ),
                    pl.BlockSpec((1, 1, features, features), lambda b, t, s, o: (t, b, 0, 0)),
                    pl.BlockSpec((1, sens, features), lambda b, t, s, o: (b, 0, 0)),
                ],
                out_specs=pl.BlockSpec(
                    (1, pieces, rows, width), lambda b, t, s, o: (b, 0, 0, 0)
                ),
                scratch_shapes=[
                    pltpu.VMEM((features * half, lanes), f32),
                    pltpu.VMEM((features, half * lanes), bf16),
                ],
            ),
            cost_estimate=cost(2 * buckets * dates * rows * features * half * lanes // 2, 2**24),
            name="local",
        )(scales, octet, shocks, transition, readout)

    operators_other = lax.ppermute(operators, "date", swap)
    discount = (step_days.astype(f32) / 365.0)[:, None, None] * discount
    discount_other = lax.ppermute(discount, "date", swap)
    sent = local(1 - core_flag)
    late_half = lax.ppermute(sent, "date", swap)

    block3 = lambda r: pl.BlockSpec((1, r, features), lambda b: (b, 0, 0))
    block, seer, late = pl.pallas_call(
        join_operator_kernel,
        out_shape=(
            jax.ShapeDtypeStruct((buckets, features, features), bf16),
            jax.ShapeDtypeStruct((buckets, 2 * seen_rows, features), bf16),
            jax.ShapeDtypeStruct((buckets, rows, features), bf16),
        ),
        grid=(buckets,),
        in_specs=[smem, block3(rows), block3(rows)],
        out_specs=(block3(features), block3(2 * seen_rows), block3(rows)),
        cost_estimate=cost(2 * buckets * rows * features**2, 2**22),
        name="join_operators",
    )(core_flag, operators, operators_other)

    combiners = []
    eye = jnp.broadcast_to(jnp.eye(features, dtype=bf16), (buckets, features, features))
    prefix = eye
    for s in range(stages - 1):
        far = [(i, i ^ (2 << s)) for i in range(segments)]
        rows_half = features // 2
        part = lax.dynamic_slice_in_dim(block, core * rows_half, rows_half, 1)
        part = lax.ppermute(part, "date", far)
        part_other = lax.ppermute(part, "date", swap)
        first = core == 0
        other = jnp.concatenate(
            [jnp.where(first, part, part_other), jnp.where(first, part_other, part)], axis=1
        )
        up = ups[s][0] == 1
        combiners.append(jnp.where(up, block, other))
        if s == 0:
            prefix = jnp.where(up, other, eye)
        else:
            moved = jnp.einsum("bij,bjk->bik", prefix, other, preferred_element_type=f32)
            prefix = jnp.where(up, moved.astype(bf16), prefix)
        if s < stages - 2:
            above = jnp.where(up, block, other)
            below = jnp.where(up, other, block)
            block = jnp.einsum(
                "bij,bjk->bik", above, below, preferred_element_type=f32
            ).astype(bf16)

    own = local(core_flag)

    ends = []
    seens = []
    for b in range(buckets):
        piece = pl.BlockSpec((1, 1, rows, width), lambda q, b=b: (b, q, 0, 0))
        result = pl.pallas_call(
            join_state_kernel,
            out_shape=(jax.ShapeDtypeStruct((pieces, 2 * seen_rows, width), f32),)
            + (jax.ShapeDtypeStruct((features, width), bf16),) * pieces,
            grid=(pieces,),
            in_specs=[
                smem,
                piece,
                piece,
                pl.BlockSpec((1, rows, features), lambda q, b=b: (b, 0, 0)),
            ],
            out_specs=(pl.BlockSpec((1, 2 * seen_rows, width), lambda q: (q, 0, 0)),)
            + (pl.BlockSpec((features, width), lambda q: (0, 0)),) * pieces,
            cost_estimate=cost(2 * rows * features * half * lanes, 2**22),
            name="join_states",
        )(core_flag, own, late_half, late)
        seens.append(result[0])
        ends.extend(result[1:])

    weight_column = risk_weight[:, :, None]
    flat = pl.BlockSpec((features, width), lambda i: (0, 0))
    count = buckets * pieces

    def stage(j, up, mine, other, combiner):
        b = j // pieces
        return pl.pallas_call(
            stage_kernel,
            out_shape=jax.ShapeDtypeStruct((features, width), bf16),
            grid=(1,),
            in_specs=[
                smem,
                flat,
                flat,
                pl.BlockSpec((1, features, features), lambda i: (b, 0, 0)),
            ],
            out_specs=flat,
            cost_estimate=cost(2 * features**2 * width, 2**20),
            name="stage",
        )(up, mine, other, combiner)

    def final(j, up, first, last, operator):
        b, q = divmod(j, pieces)
        return pl.pallas_call(
            functools.partial(final_kernel, 2 * dates),
            out_shape=jax.ShapeDtypeStruct((2, 2 * dates, width), f32),
            grid=(1,),
            in_specs=[
                smem,
                flat,
                flat,
                pl.BlockSpec((1, features, features), lambda i: (b, 0, 0)),
                pl.BlockSpec((1, 2 * seen_rows, features), lambda i: (b, 0, 0)),
                pl.BlockSpec((1, 2 * seen_rows, width), lambda i: (q, 0, 0)),
                pl.BlockSpec((1, sens, 1), lambda i: (b, 0, 0)),
                pl.BlockSpec((1, sens, sens), lambda i: (b, 0, 0)),
            ],
            out_specs=pl.BlockSpec((2, 2 * dates, width), lambda i: (0, 0, 0)),
            cost_estimate=cost(4 * features**2 * width, 2**21),
            name="final",
        )(up, first, last, operator, seer, seens[b], weight_column, correlation)

    always = jnp.ones((1,), jnp.int32)
    hold = [jnp.zeros((features, width), bf16)] * count
    hold_flag = always
    for s in range(stages):
        last = s == stages - 1
        bit = 2 << s
        link = [(i, i ^ bit) for i in range(segments) if not (last and i & bit)]
        arrived = []
        for j in range(count):
            leaving = ends[j]
            if j >= flight:
                leaving, arrived[j - flight] = lax.optimization_barrier(
                    (leaving, arrived[j - flight])
                )
            arrived.append(lax.ppermute(leaving, "date", link))
        if last:
            results = [final(j, hold_flag, hold[j], arrived[j], prefix) for j in range(count)]
        else:
            if s == 0:
                hold = arrived
                hold_flag = ups[0]
            else:
                raise_by = [
                    hold[j].astype(f32)
                    + dot(prefix[j // pieces], arrived[j])
                    for j in range(count)
                ]
                hold = [jnp.where(ups[s][0] == 1, r, h).astype(bf16) for r, h in zip(raise_by, hold)]
            ends = [stage(j, ups[s], ends[j], arrived[j], combiners[s]) for j in range(count)]

    stats = jnp.stack(results).reshape(buckets, pieces, 2, 2 * dates, pair, lanes)
    stats = jnp.moveaxis(stats, 2, 0)
    stats = jnp.moveaxis(stats, 3, 2).reshape(2, buckets, 2 * dates, half, lanes)
    local_micro = discount.shape[1]
    both = jnp.where(
        core == 0,
        jnp.stack([discount, discount_other]),
        jnp.stack([discount_other, discount]),
    )
    body = jnp.concatenate([jnp.sum(stats[0], axis=0, keepdims=True), stats[1]], axis=0)
    message = jnp.concatenate([body.reshape(-1, lanes), both.reshape(-1, lanes)], axis=0)
    gathered = [message]
    for k in range(1, zs):
        gathered.append(lax.ppermute(message, "bucket", [(i, (i + k) % zs) for i in range(zs)]))
    gathered = jnp.roll(jnp.stack(gathered[::-1]), z + 1, axis=0)
    body_rows = body.size // lanes
    parts = gathered[:, :body_rows].reshape(zs, buckets + 1, 2 * dates, half, lanes)
    discounts = gathered[:, body_rows:].reshape(zs, 2 * dates, local_micro, lanes)
    discounts = jnp.swapaxes(discounts, 0, 1).reshape(2 * dates, batches, lanes)
    discounts = lax.dynamic_slice_in_dim(discounts, core * half, half, 1)
    within = jnp.sum(parts[:, 0], axis=0)
    nets = parts[:, 1:].reshape(zs * buckets, 2 * dates, half, lanes)
    gamma = (
        0.5
        * (cross_gamma + cross_gamma.T)
        * (1.0 - jnp.eye(cross_gamma.shape[0], dtype=f32))
    )
    coupled = jnp.sum(gamma[:, :, None, None, None] * nets[None], axis=1)
    squares = within + jnp.sum(nets * coupled, axis=0)
    counts = lax.dynamic_slice_in_dim(path_counts, core * half, half)
    alive = jnp.arange(lanes, dtype=jnp.int32)[None, :] < counts[:, None]
    margins = jnp.where(alive[None], jnp.sqrt(squares), f32(0.0))
    total = jnp.sum(discounts * margins / counts.astype(f32)[None, :, None])
    start = z * local_micro
    holder = start // half
    inside = start - holder * half
    block_of = lambda section: lax.dynamic_slice(
        margins, (section * dates, inside, 0), (dates, local_micro, lanes)
    )
    out = jnp.concatenate(
        [block_of(1 - core).reshape(-1, lanes), jnp.full((8, lanes), total)], axis=0
    )
    came = lax.ppermute(out, "date", swap)
    split_row = dates * local_micro
    margin = jnp.where(
        holder == core, block_of(core), came[:split_row].reshape(dates, local_micro, lanes)
    )
    total = jnp.full((8, lanes), total) + came[split_row:]
    step = 2
    while step < segments:
        total = total + lax.ppermute(total, "date", [(i, i ^ step) for i in range(segments)])
        step *= 2
    return (margin, total[0, 0])


def solution(mesh):
    in_specs = (
        P("date", "bucket", None, None),
        P("date", "bucket", None, None, None),
        P("date"),
        P("bucket", None, None),
        P("bucket", None),
        P("bucket", None, None),
        P(),
        P("date", "bucket", None),
        P(),
    )
    out_specs = (P("date", "bucket", None), P())
    return jax.shard_map(shards, mesh=mesh, in_specs=in_specs, out_specs=out_specs, check_vma=False)
```

```python
import functools

import jax
import jax.numpy as jnp
from jax import lax
from jax.experimental import pallas as pl
from jax.experimental.pallas import tpu as pltpu
from jax.sharding import PartitionSpec as P

epsilon = 1e-06
f32 = jnp.float32
bf16 = jnp.bfloat16
pair = 2
flight = 3
lag = 2


def dot(a, b):
    return jnp.dot(a, b, preferred_element_type=f32)


def split(x):
    high = x.astype(bf16)
    return high, (x - high.astype(f32)).astype(bf16)


def cost(flops, read):
    return pl.CostEstimate(flops=flops, bytes_accessed=read, transcendentals=0)


def operator_kernel(dates, a_ref, r_ref, w_ref):
    features = a_ref.shape[-1]
    sens = r_ref.shape[1]
    product = a_ref[0, 0]
    for t in range(dates):
        if t:
            product = dot(a_ref[t, 0], product).astype(bf16)
        row = features + t * sens
        w_ref[0, row : row + sens, :] = dot(r_ref[0], product).astype(bf16)
    w_ref[0, :features, :] = product


def local_kernel(scale_ref, octet_ref, x_ref, a_ref, r_ref, out_ref, rows_ref, state_ref):
    features, micro, lanes = x_ref.shape[2:]
    sens = r_ref.shape[1]
    t = pl.program_id(1)
    rows_ref[...] = x_ref[0, 0].astype(f32).reshape(features * micro, lanes)
    scale = scale_ref[t]
    width = pair * lanes

    def shock(q):
        return scale * jnp.concatenate(
            [rows_ref[pl.ds(q * pair + i, features, stride=micro), :] for i in range(pair)],
            axis=1,
        )

    @pl.when(t == 0)
    def _():
        for q in range(micro // pair):
            state_ref[:, q * width : (q + 1) * width] = shock(q).astype(bf16)

    @pl.when(t > 0)
    def _():
        for q in range(micro // pair):
            cols = slice(q * width, (q + 1) * width)
            state_ref[:, cols] = (shock(q) + dot(a_ref[0, 0], state_ref[:, cols])).astype(bf16)

    row = pl.multiple_of(features + t * sens, sens)
    for q in range(micro // pair):
        state = state_ref[:, q * width : (q + 1) * width]
        out_ref[0, q, pl.ds(row, sens), :] = dot(r_ref[0], state).astype(bf16)

    @pl.when(t == pl.num_programs(1) - 1)
    def _():
        for q in range(micro // pair):
            out_ref[0, q, :features, :] = state_ref[:, q * width : (q + 1) * width]


def join_operator_kernel(core_ref, mine_ref, other_ref, p_ref, q_ref, late_ref):
    features = mine_ref.shape[2]
    first = core_ref[0] == 0
    mine, other = mine_ref[0], other_ref[0]
    early = jnp.where(first, mine, other)
    late = jnp.where(first, other, mine)
    joined = dot(late, early[:features]).astype(bf16)
    p_ref[0] = joined[:features]
    seen = late.shape[0] - features
    q_ref[0, :seen, :] = early[features:]
    q_ref[0, seen:, :] = joined[features:]
    late_ref[0] = late


def join_state_kernel(b, core_ref, mine_ref, other_ref, late_ref, seen_ref, *end_refs):
    features = late_ref.shape[2]
    first = core_ref[0] == 0
    late_operator = late_ref[b]
    for q, end_ref in enumerate(end_refs):
        mine, other = mine_ref[0, q], other_ref[0, q]
        early = jnp.where(first, mine, other)
        late = jnp.where(first, other, mine)
        joined = dot(late_operator, early[:features]) + late.astype(f32)
        seen = late.shape[0] - features
        seen_ref[q, :seen, :] = early[features:].astype(f32)
        seen_ref[q, seen:, :] = joined[features:]
        end_ref[...] = joined[:features].astype(bf16)


def stage_kernel(b, up_ref, mine_ref, other_ref, a_ref, out_ref):
    up = up_ref[0] == 1
    mine, other = mine_ref[...], other_ref[...]
    early = jnp.where(up, other, mine)
    late = jnp.where(up, mine, other)
    out_ref[...] = (dot(a_ref[b], early) + late.astype(f32)).astype(bf16)


def final_kernel(
    b, q, dates, up_ref, first_ref, last_ref, phi_ref, q_ref, seen_ref, rw_ref, c_ref, out_ref
):
    sens = rw_ref.shape[1]
    width = first_ref.shape[1]
    first = first_ref[...].astype(f32)
    first = jnp.where(up_ref[0] == 1, first, jnp.zeros_like(first))
    entering = (first + dot(phi_ref[b], last_ref[...])).astype(bf16)
    seen = seen_ref[q] + dot(q_ref[b], entering)
    weight = rw_ref[b]
    ws = jnp.concatenate(
        [weight * seen[t * sens : (t + 1) * sens] for t in range(dates)], axis=1
    )
    c_high, c_low = split(c_ref[b])
    w_high, w_low = split(ws)
    mixed = dot(
        jnp.concatenate([c_high, c_low, c_high], axis=1),
        jnp.concatenate([w_high, w_high, w_low], axis=0),
    )
    within = jnp.sum(ws * mixed, axis=0, keepdims=True) + epsilon
    root = jnp.sqrt(within)
    net = jnp.clip(jnp.sum(ws, axis=0, keepdims=True), -root, root)
    for t in range(dates):
        out_ref[0, t : t + 1, :] = within[:, t * width : (t + 1) * width]
        out_ref[1, t : t + 1, :] = net[:, t * width : (t + 1) * width]


def pack_kernel(buckets, pieces, *refs):
    stats, discount_ref, out_ref = refs[:-2], refs[-2], refs[-1]
    dates = stats[0].shape[1]
    lanes = out_ref.shape[1]
    block = pair * dates
    for q in range(pieces):
        own = [stats[b * pieces + q] for b in range(buckets)]
        within = sum(ref[0] for ref in own)
        for r, value in enumerate([within] + [ref[1] for ref in own]):
            rows = jnp.concatenate(
                [value[:, i * lanes : (i + 1) * lanes] for i in range(pair)], axis=0
            )
            row = (r * pieces + q) * block
            out_ref[row : row + block, :] = rows.astype(bf16)
    out_ref[(buckets + 1) * pieces * block :, :] = discount_ref[...]


def margin_kernel(
    buckets, dates, local_micro, half, place_ref, gamma_ref, count_ref, *refs
):
    messages, (out_ref, spread_ref, margin_ref) = refs[:-3], refs[-3:]
    zs = len(messages)
    lanes = out_ref.shape[2]
    body = half * dates
    shard, core = place_ref[0], place_ref[1]
    origin = [lax.rem(shard - k + zs, zs) for k in range(zs)]
    within = 0.0
    nets = []
    for k, ref in enumerate(messages):
        within = within + ref[:body, :].astype(f32)
        for b in range(buckets):
            row = (b + 1) * body
            nets.append((origin[k] * buckets + b, ref[row : row + body, :].astype(f32)))
        row = (buckets + 1) * body
        size = local_micro * dates
        rest = ref[row : row + 2 * size, :].astype(f32)
        spread_ref[pl.ds(origin[k] * local_micro, local_micro)] = (
            rest[:size] + rest[size:]
        ).reshape(local_micro, dates, lanes)
    squares = within
    for i, (at, net) in enumerate(nets):
        coupled = 0.0
        for k, (other_at, other) in enumerate(nets):
            if k != i:
                coupled = coupled + gamma_ref[at, other_at] * other
        squares = squares + net * coupled
    root = jnp.sqrt(squares).reshape(half, dates, lanes)
    lane = lax.broadcasted_iota(jnp.int32, (dates, lanes), 1)
    total = jnp.zeros((dates, lanes), f32)
    for m in range(half):
        live = count_ref[core * half + m]
        margin = jnp.where(lane < live, root[m], f32(0.0))
        margin_ref[m] = margin
        total = total + spread_ref[core * half + m] * margin / live.astype(f32)
    total = jnp.sum(jnp.sum(total, axis=0, keepdims=True), axis=1, keepdims=True)
    out_ref[:local_micro] = margin_ref[pl.ds(place_ref[2], local_micro)]
    out_ref[local_micro] = jnp.broadcast_to(total, (dates, lanes))


def shards(
    transition,
    shocks,
    step_days,
    readout,
    risk_weight,
    correlation,
    cross_gamma,
    discount,
    path_counts,
):
    position = lax.axis_index("date")
    segments = lax.axis_size("date")
    zs = lax.axis_size("bucket")
    z = lax.axis_index("bucket")
    dates, buckets, features, batches, lanes = shocks.shape
    sens = readout.shape[1]
    scales = jnp.sqrt(step_days.astype(f32) / 30.0)
    half = batches // 2
    pieces = half // pair
    width = pair * lanes
    seen_rows = dates * sens
    rows = features + seen_rows
    core = lax.rem(position, 2)
    core_flag = core.astype(jnp.int32).reshape(1)
    stages = (segments // 2).bit_length() - 1
    ups = [lax.rem(position // (2 << s), 2).astype(jnp.int32).reshape(1) for s in range(stages)]
    swap = [(i, i ^ 1) for i in range(segments)]
    smem = pl.BlockSpec(memory_space=pltpu.SMEM)

    operators = pl.pallas_call(
        functools.partial(operator_kernel, dates),
        out_shape=jax.ShapeDtypeStruct((buckets, rows, features), bf16),
        grid=(buckets,),
        in_specs=[
            pl.BlockSpec((dates, 1, features, features), lambda b: (0, b, 0, 0)),
            pl.BlockSpec((1, sens, features), lambda b: (b, 0, 0)),
        ],
        out_specs=pl.BlockSpec((1, rows, features), lambda b: (b, 0, 0)),
        cost_estimate=cost(2 * buckets * dates * features**3, 2**23),
        compiler_params=pltpu.CompilerParams(vmem_limit_bytes=24 * 2**20),
        name="operators",
    )(transition, readout)

    def local(octet, scales):
        return pl.pallas_call(
            local_kernel,
            out_shape=jax.ShapeDtypeStruct((buckets, pieces, rows, width), bf16),
            grid_spec=pltpu.PrefetchScalarGridSpec(
                num_scalar_prefetch=2,
                grid=(buckets, dates),
                in_specs=[
                    pl.BlockSpec(
                        (1, 1, features, half, lanes), lambda b, t, s, o: (t, b, 0, o[0], 0)
                    ),
                    pl.BlockSpec((1, 1, features, features), lambda b, t, s, o: (t, b, 0, 0)),
                    pl.BlockSpec((1, sens, features), lambda b, t, s, o: (b, 0, 0)),
                ],
                out_specs=pl.BlockSpec(
                    (1, pieces, rows, width), lambda b, t, s, o: (b, 0, 0, 0)
                ),
                scratch_shapes=[
                    pltpu.VMEM((features * half, lanes), f32),
                    pltpu.VMEM((features, half * lanes), bf16),
                ],
            ),
            compiler_params=pltpu.CompilerParams(vmem_limit_bytes=24 * 2**20),
            cost_estimate=cost(2 * buckets * dates * rows * features * half * lanes // 2, 2**24),
            name="local",
        )(scales, octet, shocks, transition, readout)

    scales, operators = lax.optimization_barrier((scales, operators))
    operators_other = lax.ppermute(operators, "date", swap)
    discount = (step_days.astype(f32) / 365.0)[:, None, None] * discount
    discount_other = lax.ppermute(discount, "date", swap)
    sent = local(1 - core_flag, scales)
    operators_other, sent = lax.optimization_barrier((operators_other, sent))
    late_half = lax.ppermute(sent, "date", swap)

    block3 = lambda r: pl.BlockSpec((1, r, features), lambda b: (b, 0, 0))
    block, seer, late = pl.pallas_call(
        join_operator_kernel,
        out_shape=(
            jax.ShapeDtypeStruct((buckets, features, features), bf16),
            jax.ShapeDtypeStruct((buckets, 2 * seen_rows, features), bf16),
            jax.ShapeDtypeStruct((buckets, rows, features), bf16),
        ),
        grid=(buckets,),
        in_specs=[smem, block3(rows), block3(rows)],
        out_specs=(block3(features), block3(2 * seen_rows), block3(rows)),
        cost_estimate=cost(2 * buckets * rows * features**2, 2**22),
        compiler_params=pltpu.CompilerParams(vmem_limit_bytes=24 * 2**20),
        name="join_operators",
    )(core_flag, operators, operators_other)

    combiners = []
    eye = jnp.broadcast_to(jnp.eye(features, dtype=bf16), (buckets, features, features))
    prefix = eye
    for s in range(stages - 1):
        far = [(i, i ^ (2 << s)) for i in range(segments)]
        rows_half = features // 2
        part = lax.dynamic_slice_in_dim(block, core * rows_half, rows_half, 1)
        if s == 0:
            scales, part = lax.optimization_barrier((scales, part))
        part = lax.ppermute(part, "date", far)
        if s == 0:
            own = local(core_flag, scales)
            part, own = lax.optimization_barrier((part, own))
        part_other = lax.ppermute(part, "date", swap)
        first = core == 0
        other = jnp.concatenate(
            [jnp.where(first, part, part_other), jnp.where(first, part_other, part)], axis=1
        )
        up = ups[s][0] == 1
        combiners.append(jnp.where(up, block, other))
        if s == 0:
            prefix = jnp.where(up, other, eye)
        else:
            moved = jnp.einsum("bij,bjk->bik", prefix, other, preferred_element_type=f32)
            prefix = jnp.where(up, moved.astype(bf16), prefix)
        if s < stages - 2:
            above = jnp.where(up, block, other)
            below = jnp.where(up, other, block)
            block = jnp.einsum(
                "bij,bjk->bik", above, below, preferred_element_type=f32
            ).astype(bf16)

    if stages < 2:
        own = local(core_flag, scales)

    ends = []
    seens = []
    vmem = pl.BlockSpec(memory_space=pltpu.VMEM)
    small = pltpu.CompilerParams(vmem_limit_bytes=16 * 2**20)
    for b in range(buckets):
        piece = pl.BlockSpec((1, pieces, rows, width), lambda i, b=b: (b, 0, 0, 0))
        result = pl.pallas_call(
            functools.partial(join_state_kernel, b),
            out_shape=(jax.ShapeDtypeStruct((pieces, 2 * seen_rows, width), f32),)
            + (jax.ShapeDtypeStruct((features, width), bf16),) * pieces,
            grid=(1,),
            in_specs=[smem, piece, piece, vmem],
            out_specs=(vmem,) * (pieces + 1),
            compiler_params=small,
            cost_estimate=cost(2 * rows * features * half * lanes, 2**22),
            name="join_states",
        )(core_flag, own, late_half, late)
        seens.append(result[0])
        ends.extend(result[1:])

    weight_column = risk_weight[:, :, None]
    count = buckets * pieces

    def stage(j, up, mine, other, combiner):
        return pl.pallas_call(
            functools.partial(stage_kernel, j // pieces),
            out_shape=jax.ShapeDtypeStruct((features, width), bf16),
            in_specs=[smem, vmem, vmem, vmem],
            out_specs=vmem,
            compiler_params=small,
            cost_estimate=cost(2 * features**2 * width, 2**20),
            name="stage",
        )(up, mine, other, combiner)

    def final(j, up, first, last, operator):
        b, q = divmod(j, pieces)
        return pl.pallas_call(
            functools.partial(final_kernel, b, q, 2 * dates),
            out_shape=jax.ShapeDtypeStruct((2, 2 * dates, width), f32),
            in_specs=[smem] + [vmem] * 7,
            out_specs=vmem,
            compiler_params=small,
            cost_estimate=cost(4 * features**2 * width, 2**21),
            name="final",
        )(up, first, last, operator, seer, seens[b], weight_column, correlation)

    hold = [jnp.zeros((features, width), bf16)] * count
    hold_flag = jnp.ones((1,), jnp.int32)
    come = None
    for s in range(stages):
        last = s == stages - 1
        bit = 2 << s
        link = [(i, i ^ bit) for i in range(segments) if not (last and i & bit)]
        arrived = []
        results = []
        leaving_list = []
        for j in range(count):
            if come is None:
                leaving = ends[j]
            else:
                near = come[j]
                if last and j > lag:
                    near, results[j - lag - 1] = lax.optimization_barrier(
                        (near, results[j - lag - 1])
                    )
                leaving = stage(j, ups[s - 1], ends[j], near, combiners[s - 1])
            if j >= flight:
                leaving, arrived[j - flight] = lax.optimization_barrier(
                    (leaving, arrived[j - flight])
                )
            leaving_list.append(leaving)
            arrived.append(lax.ppermute(leaving, "date", link))
            if last and j >= lag:
                i = j - lag
                results.append(final(i, hold_flag, hold[i], arrived[i], prefix))
        if last:
            for i in range(len(results), count):
                results.append(final(i, hold_flag, hold[i], arrived[i], prefix))
        else:
            if s == 0:
                hold = arrived
                hold_flag = ups[0]
            else:
                raised = [
                    hold[j].astype(f32) + dot(prefix[j // pieces], arrived[j])
                    for j in range(count)
                ]
                hold = [jnp.where(ups[s][0] == 1, r, h).astype(bf16) for r, h in zip(raised, hold)]
            ends = leaving_list
            come = arrived

    local_micro = discount.shape[1]
    both = jnp.where(
        core == 0,
        jnp.stack([discount, discount_other]),
        jnp.stack([discount_other, discount]),
    ).reshape(2 * dates, local_micro, lanes)
    high, low = split(jnp.swapaxes(both, 0, 1))
    carried = jnp.concatenate([high.reshape(-1, lanes), low.reshape(-1, lanes)], axis=0)
    body_rows = (buckets + 1) * half * 2 * dates
    message = pl.pallas_call(
        functools.partial(pack_kernel, buckets, pieces),
        out_shape=jax.ShapeDtypeStruct((body_rows + carried.shape[0], lanes), bf16),
        in_specs=[vmem] * (count + 1),
        out_specs=vmem,
        compiler_params=small,
        name="pack",
    )(*results, carried)
    gathered = [message]
    for k in range(1, zs):
        gathered.append(lax.ppermute(message, "bucket", [(i, (i + k) % zs) for i in range(zs)]))
    gamma = (
        0.5
        * (cross_gamma + cross_gamma.T)
        * (1.0 - jnp.eye(cross_gamma.shape[0], dtype=f32))
    )
    start = z * local_micro
    holder = start // half
    place = jnp.stack([z, core, start - holder * half]).astype(jnp.int32)
    out = pl.pallas_call(
        functools.partial(margin_kernel, buckets, 2 * dates, local_micro, half),
        out_shape=jax.ShapeDtypeStruct((local_micro + 1, 2 * dates, lanes), f32),
        in_specs=[smem] * 3 + [vmem] * zs,
        out_specs=vmem,
        scratch_shapes=[
            pltpu.VMEM((batches, 2 * dates, lanes), f32),
            pltpu.VMEM((half, 2 * dates, lanes), f32),
        ],
        compiler_params=small,
        name="margins",
    )(place, gamma, path_counts, *gathered)
    came = lax.ppermute(out, "date", swap)
    margin = jnp.where(holder == core, out[:local_micro], came[:local_micro])
    margin = lax.dynamic_slice_in_dim(margin, core * dates, dates, 1)
    margin = jnp.swapaxes(margin, 0, 1)
    total = out[local_micro] + came[local_micro]
    step = 2
    while step < segments:
        total = total + lax.ppermute(total, "date", [(i, i ^ step) for i in range(segments)])
        step *= 2
    return (margin, total[0, 0])


def solution(mesh):
    in_specs = (
        P("date", "bucket", None, None),
        P("date", "bucket", None, None, None),
        P("date"),
        P("bucket", None, None),
        P("bucket", None),
        P("bucket", None, None),
        P(),
        P("date", "bucket", None),
        P(),
    )
    out_specs = (P("date", "bucket", None), P())
    return jax.shard_map(shards, mesh=mesh, in_specs=in_specs, out_specs=out_specs, check_vma=False)
```

```python
import functools

import jax
import jax.numpy as jnp
from jax import lax
from jax.experimental import pallas as pl
from jax.experimental.pallas import tpu as pltpu
from jax.sharding import PartitionSpec as P


epsilon = 1e-06
f32 = jnp.float32
bf16 = jnp.bfloat16
pair = 2
flight = 4
lag = 2
early = 2


def dot(a, b):
    return jnp.dot(a, b, preferred_element_type=f32)


def split(x):
    high = x.astype(bf16)
    return high, (x - high.astype(f32)).astype(bf16)


def cost(flops, read):
    return pl.CostEstimate(flops=flops, bytes_accessed=read, transcendentals=0)


def operator_kernel(dates, a_ref, r_ref, w_ref):
    features = a_ref.shape[-1]
    sens = r_ref.shape[1]
    product = a_ref[0, 0]
    for t in range(dates):
        if t:
            product = dot(a_ref[t, 0], product).astype(bf16)
        row = features + t * sens
        w_ref[0, row : row + sens, :] = dot(r_ref[0], product).astype(bf16)
    w_ref[0, :features, :] = product


def local_kernel(
    dates, scale_ref, octet_ref, x_ref, a_ref, r_ref, out_ref, even_ref, odd_ref, state_ref
):
    features, micro, lanes = x_ref.shape[2:]
    sens = r_ref.shape[1]
    step = pl.program_id(0)
    width = pair * lanes
    pieces = micro // pair
    chunk = features // pieces
    buffers = (even_ref, odd_ref)

    def lay_out(into, q):
        part = slice(q * chunk, (q + 1) * chunk)
        into[q * chunk * micro : (q + 1) * chunk * micro, :] = (
            x_ref[0, 0, part].astype(f32).reshape(chunk * micro, lanes)
        )

    def advance(rows_ref, q, first):
        cols = slice(q * width, (q + 1) * width)
        total = scale_ref[jnp.maximum(step - 1, 0)] * jnp.concatenate(
            [rows_ref[pl.ds(q * pair + i, features, stride=micro), :] for i in range(pair)],
            axis=1,
        )
        if not first:
            total = total + dot(a_ref[0, 0], state_ref[:, cols])
        state = total.astype(bf16)
        state_ref[:, cols] = state
        row = pl.multiple_of(features + (step - 1) * sens, sens)
        out_ref[q, pl.ds(row, sens), :] = dot(r_ref[0], state).astype(bf16)
        return state

    def both(parity, ahead, first, last):
        for q in range(pieces):
            state = advance(buffers[1 - parity], q, first)
            if ahead:
                lay_out(buffers[parity], q)
            if last:
                out_ref[q, :features, :] = state

    @pl.when(step == 0)
    def _():
        for q in range(pieces):
            lay_out(buffers[0], q)

    @pl.when(step == 1)
    def _():
        both(1, dates > 1, True, dates == 1)

    for parity in range(2):

        @pl.when((lax.rem(step, 2) == parity) & (step > 1) & (step < dates))
        def _():
            both(parity, True, False, False)

    if dates > 1:

        @pl.when(step == dates)
        def _():
            both(dates % 2, False, False, True)


def join_operator_kernel(core_ref, mine_ref, other_ref, p_ref, q_ref, late_ref):
    features = mine_ref.shape[2]
    first = core_ref[0] == 0
    mine, other = mine_ref[0], other_ref[0]
    early = jnp.where(first, mine, other)
    late = jnp.where(first, other, mine)
    joined = dot(late, early[:features]).astype(bf16)
    p_ref[0] = joined[:features]
    seen = late.shape[0] - features
    q_ref[0, :seen, :] = early[features:]
    q_ref[0, seen:, :] = joined[features:]
    late_ref[0] = late


def join_state_kernel(b, core_ref, mine_ref, other_ref, late_ref, seen_ref, *end_refs):
    features = late_ref.shape[2]
    first = core_ref[0] == 0
    late_operator = late_ref[b]
    for q, end_ref in enumerate(end_refs):
        mine, other = mine_ref[q], other_ref[q]
        early = jnp.where(first, mine, other)
        late = jnp.where(first, other, mine)
        joined = dot(late_operator, early[:features]) + late.astype(f32)
        seen = late.shape[0] - features
        seen_ref[q, :seen, :] = early[features:].astype(f32)
        seen_ref[q, seen:, :] = joined[features:]
        end_ref[...] = joined[:features].astype(bf16)


def stage_kernel(b, up_ref, mine_ref, other_ref, a_ref, out_ref):
    up = up_ref[0] == 1
    mine, other = mine_ref[...], other_ref[...]
    early = jnp.where(up, other, mine)
    late = jnp.where(up, mine, other)
    out_ref[...] = (dot(a_ref[b], early) + late.astype(f32)).astype(bf16)


def final_kernel(
    b, q, dates, up_ref, first_ref, last_ref, phi_ref, q_ref, seen_ref, rw_ref, c_ref, out_ref
):
    sens = rw_ref.shape[1]
    width = first_ref.shape[1]
    first = first_ref[...].astype(f32)
    first = jnp.where(up_ref[0] == 1, first, jnp.zeros_like(first))
    entering = (first + dot(phi_ref[b], last_ref[...])).astype(bf16)
    seen = seen_ref[q] + dot(q_ref[b], entering)
    weight = rw_ref[b]
    ws = jnp.concatenate(
        [weight * seen[t * sens : (t + 1) * sens] for t in range(dates)], axis=1
    )
    c_high, c_low = split(c_ref[b])
    w_high, w_low = split(ws)
    mixed = dot(
        jnp.concatenate([c_high, c_low, c_high], axis=1),
        jnp.concatenate([w_high, w_high, w_low], axis=0),
    )
    within = jnp.sum(ws * mixed, axis=0, keepdims=True) + epsilon
    root = jnp.sqrt(within)
    net = jnp.clip(jnp.sum(ws, axis=0, keepdims=True), -root, root)
    for t in range(dates):
        out_ref[0, t : t + 1, :] = within[:, t * width : (t + 1) * width]
        out_ref[1, t : t + 1, :] = net[:, t * width : (t + 1) * width]


def pack_kernel(buckets, pieces, *refs):
    stats, discount_ref, out_ref = refs[:-2], refs[-2], refs[-1]
    dates = stats[0].shape[1]
    lanes = out_ref.shape[1]
    block = pair * dates
    for q in range(pieces):
        own = [stats[b * pieces + q] for b in range(buckets)]
        within = sum(ref[0] for ref in own)
        for r, value in enumerate([within] + [ref[1] for ref in own]):
            rows = jnp.concatenate(
                [value[:, i * lanes : (i + 1) * lanes] for i in range(pair)], axis=0
            )
            row = (r * pieces + q) * block
            out_ref[row : row + block, :] = rows.astype(bf16)
    out_ref[(buckets + 1) * pieces * block :, :] = discount_ref[...]


def margin_kernel(
    buckets, dates, local_micro, half, place_ref, gamma_ref, count_ref, *refs
):
    messages, (out_ref, spread_ref, margin_ref) = refs[:-3], refs[-3:]
    zs = len(messages)
    lanes = out_ref.shape[2]
    body = half * dates
    shard, core = place_ref[0], place_ref[1]
    origin = [lax.rem(shard - k + zs, zs) for k in range(zs)]
    within = 0.0
    nets = []
    for k, ref in enumerate(messages):
        within = within + ref[:body, :].astype(f32)
        for b in range(buckets):
            row = (b + 1) * body
            nets.append((origin[k] * buckets + b, ref[row : row + body, :].astype(f32)))
        row = (buckets + 1) * body
        size = local_micro * dates
        rest = ref[row : row + 2 * size, :].astype(f32)
        spread_ref[pl.ds(origin[k] * local_micro, local_micro)] = (
            rest[:size] + rest[size:]
        ).reshape(local_micro, dates, lanes)
    squares = within
    for i, (at, net) in enumerate(nets):
        coupled = 0.0
        for k, (other_at, other) in enumerate(nets):
            if k != i:
                coupled = coupled + gamma_ref[at, other_at] * other
        squares = squares + net * coupled
    root = jnp.sqrt(squares).reshape(half, dates, lanes)
    lane = lax.broadcasted_iota(jnp.int32, (dates, lanes), 1)
    total = jnp.zeros((dates, lanes), f32)
    for m in range(half):
        live = count_ref[core * half + m]
        margin = jnp.where(lane < live, root[m], f32(0.0))
        margin_ref[m] = margin
        total = total + spread_ref[core * half + m] * margin / live.astype(f32)
    total = jnp.sum(jnp.sum(total, axis=0, keepdims=True), axis=1, keepdims=True)
    out_ref[:local_micro] = margin_ref[pl.ds(place_ref[2], local_micro)]
    out_ref[local_micro] = jnp.broadcast_to(total, (dates, lanes))


def shards(
    transition,
    shocks,
    step_days,
    readout,
    risk_weight,
    correlation,
    cross_gamma,
    discount,
    path_counts,
):
    position = lax.axis_index("date")
    segments = lax.axis_size("date")
    zs = lax.axis_size("bucket")
    z = lax.axis_index("bucket")
    dates, buckets, features, batches, lanes = shocks.shape
    sens = readout.shape[1]
    scales = jnp.sqrt(step_days.astype(f32) / 30.0)
    half = batches // 2
    pieces = half // pair
    width = pair * lanes
    seen_rows = dates * sens
    rows = features + seen_rows
    core = lax.rem(position, 2)
    core_flag = core.astype(jnp.int32).reshape(1)
    stages = (segments // 2).bit_length() - 1
    ups = [lax.rem(position // (2 << s), 2).astype(jnp.int32).reshape(1) for s in range(stages)]
    swap = [(i, i ^ 1) for i in range(segments)]
    smem = pl.BlockSpec(memory_space=pltpu.SMEM)

    operators = pl.pallas_call(
        functools.partial(operator_kernel, dates),
        out_shape=jax.ShapeDtypeStruct((buckets, rows, features), bf16),
        grid=(buckets,),
        in_specs=[
            pl.BlockSpec((dates, 1, features, features), lambda b: (0, b, 0, 0)),
            pl.BlockSpec((1, sens, features), lambda b: (b, 0, 0)),
        ],
        out_specs=pl.BlockSpec((1, rows, features), lambda b: (b, 0, 0)),
        cost_estimate=cost(2 * buckets * dates * features**3, 2**23),
        compiler_params=pltpu.CompilerParams(vmem_limit_bytes=50 * 2**20),
        name="operators",
    )(transition, readout)

    def local(b, octet, scales):
        return pl.pallas_call(
            functools.partial(local_kernel, dates),
            out_shape=jax.ShapeDtypeStruct((pieces, rows, width), bf16),
            grid_spec=pltpu.PrefetchScalarGridSpec(
                num_scalar_prefetch=2,
                grid=(dates + 1,),
                in_specs=[
                    pl.BlockSpec(
                        (1, 1, features, half, lanes),
                        lambda i, s, o: (jnp.minimum(i, dates - 1), b, 0, o[0], 0),
                    ),
                    pl.BlockSpec(
                        (1, 1, features, features),
                        lambda i, s, o: (jnp.maximum(i - 1, 0), b, 0, 0),
                    ),
                    pl.BlockSpec((1, sens, features), lambda i, s, o: (b, 0, 0)),
                ],
                out_specs=pl.BlockSpec((pieces, rows, width), lambda i, s, o: (0, 0, 0)),
                scratch_shapes=[
                    pltpu.VMEM((features * half, lanes), f32),
                    pltpu.VMEM((features * half, lanes), f32),
                    pltpu.VMEM((features, half * lanes), bf16),
                ],
            ),
            compiler_params=pltpu.CompilerParams(vmem_limit_bytes=50 * 2**20),
            cost_estimate=cost(2 * dates * rows * features * half * lanes // 2, 2**23),
            name="local",
        )(scales, octet, shocks, transition, readout)

    scales, operators = lax.optimization_barrier((scales, operators))
    operators_other = lax.ppermute(operators, "date", swap)
    discount = (step_days.astype(f32) / 365.0)[:, None, None] * discount
    discount_other = lax.ppermute(discount, "date", swap)
    sent = local(0, 1 - core_flag, scales)
    operators_other, sent = lax.optimization_barrier((operators_other, sent))
    late_half = lax.ppermute(sent, "date", swap)

    block3 = lambda r: pl.BlockSpec((1, r, features), lambda b: (b, 0, 0))
    block, seer, late = pl.pallas_call(
        join_operator_kernel,
        out_shape=(
            jax.ShapeDtypeStruct((buckets, features, features), bf16),
            jax.ShapeDtypeStruct((buckets, 2 * seen_rows, features), bf16),
            jax.ShapeDtypeStruct((buckets, rows, features), bf16),
        ),
        grid=(buckets,),
        in_specs=[smem, block3(rows), block3(rows)],
        out_specs=(block3(features), block3(2 * seen_rows), block3(rows)),
        cost_estimate=cost(2 * buckets * rows * features**2, 2**22),
        compiler_params=pltpu.CompilerParams(vmem_limit_bytes=50 * 2**20),
        name="join_operators",
    )(core_flag, operators, operators_other)

    combiners = []
    eye = jnp.broadcast_to(jnp.eye(features, dtype=bf16), (buckets, features, features))
    prefix = eye
    prefixes = [eye]
    for s in range(stages - 1):
        far = [(i, i ^ (2 << s)) for i in range(segments)]
        rows_half = features // 2
        part = lax.dynamic_slice_in_dim(block, core * rows_half, rows_half, 1)
        if s == 0:
            scales, part = lax.optimization_barrier((scales, part))
        part = lax.ppermute(part, "date", far)
        if s == 0:
            own = local(0, core_flag, scales)
            part, own = lax.optimization_barrier((part, own))
        part_other = lax.ppermute(part, "date", swap)
        first = core == 0
        other = jnp.concatenate(
            [jnp.where(first, part, part_other), jnp.where(first, part_other, part)], axis=1
        )
        up = ups[s][0] == 1
        combiners.append(jnp.where(up, block, other))
        if s == 0:
            prefix = jnp.where(up, other, eye)
        else:
            moved = jnp.einsum("bij,bjk->bik", prefix, other, preferred_element_type=f32)
            prefix = jnp.where(up, moved.astype(bf16), prefix)
        prefixes.append(prefix)
        if s < stages - 2:
            above = jnp.where(up, block, other)
            below = jnp.where(up, other, block)
            block = jnp.einsum(
                "bij,bjk->bik", above, below, preferred_element_type=f32
            ).astype(bf16)

    if stages < 2:
        own = local(0, core_flag, scales)

    ends = []
    seens = []
    vmem = pl.BlockSpec(memory_space=pltpu.VMEM)
    small = pltpu.CompilerParams(vmem_limit_bytes=16 * 2**20)

    def join_states(b, own, late_half):
        result = pl.pallas_call(
            functools.partial(join_state_kernel, b),
            out_shape=(jax.ShapeDtypeStruct((pieces, 2 * seen_rows, width), f32),)
            + (jax.ShapeDtypeStruct((features, width), bf16),) * pieces,
            in_specs=[smem, vmem, vmem, vmem],
            out_specs=(vmem,) * (pieces + 1),
            compiler_params=small,
            cost_estimate=cost(2 * rows * features * half * lanes, 2**22),
            name="join_states",
        )(core_flag, own, late_half, late)
        seens.append(result[0])
        ends.extend(result[1:])

    weight_column = risk_weight[:, :, None]
    count = buckets * pieces

    def stage(j, up, mine, other, combiner):
        return pl.pallas_call(
            functools.partial(stage_kernel, j // pieces),
            out_shape=jax.ShapeDtypeStruct((features, width), bf16),
            in_specs=[smem, vmem, vmem, vmem],
            out_specs=vmem,
            compiler_params=small,
            cost_estimate=cost(2 * features**2 * width, 2**20),
            name="stage",
        )(up, mine, other, combiner)

    def final(j, up, first, last, operator):
        b, q = divmod(j, pieces)
        return pl.pallas_call(
            functools.partial(final_kernel, b, q, 2 * dates),
            out_shape=jax.ShapeDtypeStruct((2, 2 * dates, width), f32),
            in_specs=[smem] + [vmem] * 7,
            out_specs=vmem,
            compiler_params=small,
            cost_estimate=cost(4 * features**2 * width, 2**21),
            name="final",
        )(up, first, last, operator, seer, seens[b], weight_column, correlation)

    arrived = [[] for _ in range(stages)]
    leaving = [[] for _ in range(stages)]
    holds = {}
    results = []

    def held(s, j):
        if s == 0:
            return jnp.zeros((features, width), bf16), jnp.ones((1,), jnp.int32)
        if s == 1:
            return arrived[0][j], ups[0]
        if (s, j) not in holds:
            before, flag = held(s - 1, j)
            before = jnp.where(flag[0] == 1, before, jnp.zeros_like(before)).astype(f32)
            moved = dot(prefixes[s - 1][j // pieces], arrived[s - 1][j])
            value = jnp.where(ups[s - 1][0] == 1, before + moved, before)
            holds[s, j] = value.astype(bf16)
        return holds[s, j], jnp.ones((1,), jnp.int32)

    def advance(s, after=None):
        j = len(arrived[s])
        last = s == stages - 1
        bit = 2 << s
        link = [(i, i ^ bit) for i in range(segments) if not (last and i & bit)]
        if s == 0:
            out = ends[j]
        else:
            near = arrived[s - 1][j]
            if after is not None:
                near, results[after] = lax.optimization_barrier((near, results[after]))
            out = stage(j, ups[s - 1], leaving[s - 1][j], near, combiners[s - 1])
        if j >= flight:
            out, arrived[s][j - flight] = lax.optimization_barrier((out, arrived[s][j - flight]))
        leaving[s].append(out)
        arrived[s].append(lax.ppermute(out, "date", link))

    def finish():
        i = len(results)
        before, flag = held(stages - 1, i)
        results.append(final(i, flag, before, arrived[-1][i], prefixes[stages - 1]))

    join_states(0, own, late_half)
    for b in range(buckets):
        for _ in range(pieces):
            advance(0)
        if b + 1 < buckets:
            scales, ends[-1] = lax.optimization_barrier((scales, ends[-1]))
            sent = local(b + 1, 1 - core_flag, scales)
            late_half = lax.ppermute(sent, "date", swap)
            if stages > 1:
                for _ in range(early):
                    arrived[0][len(arrived[1])], sent = lax.optimization_barrier(
                        (arrived[0][len(arrived[1])], sent)
                    )
                    advance(1)
                    scales, leaving[1][-1] = lax.optimization_barrier((scales, leaving[1][-1]))
            else:
                scales, sent = lax.optimization_barrier((scales, sent))
            own = local(b + 1, core_flag, scales)
            join_states(b + 1, own, late_half)
    for s in range(1, stages):
        last = s == stages - 1
        while len(arrived[s]) < count:
            j = len(arrived[s])
            while last and len(results) < j - lag:
                finish()
            advance(s, j - lag - 1 if last and j > lag else None)
    while len(results) < count:
        finish()

    local_micro = discount.shape[1]
    both = jnp.where(
        core == 0,
        jnp.stack([discount, discount_other]),
        jnp.stack([discount_other, discount]),
    ).reshape(2 * dates, local_micro, lanes)
    high, low = split(jnp.swapaxes(both, 0, 1))
    carried = jnp.concatenate([high.reshape(-1, lanes), low.reshape(-1, lanes)], axis=0)
    body_rows = (buckets + 1) * half * 2 * dates
    message = pl.pallas_call(
        functools.partial(pack_kernel, buckets, pieces),
        out_shape=jax.ShapeDtypeStruct((body_rows + carried.shape[0], lanes), bf16),
        in_specs=[vmem] * (count + 1),
        out_specs=vmem,
        compiler_params=small,
        name="pack",
    )(*results, carried)
    gathered = [message]
    for k in range(1, zs):
        gathered.append(lax.ppermute(message, "bucket", [(i, (i + k) % zs) for i in range(zs)]))
    gamma = (
        0.5
        * (cross_gamma + cross_gamma.T)
        * (1.0 - jnp.eye(cross_gamma.shape[0], dtype=f32))
    )
    start = z * local_micro
    holder = start // half
    place = jnp.stack([z, core, start - holder * half]).astype(jnp.int32)
    out = pl.pallas_call(
        functools.partial(margin_kernel, buckets, 2 * dates, local_micro, half),
        out_shape=jax.ShapeDtypeStruct((local_micro + 1, 2 * dates, lanes), f32),
        in_specs=[smem] * 3 + [vmem] * zs,
        out_specs=vmem,
        scratch_shapes=[
            pltpu.VMEM((batches, 2 * dates, lanes), f32),
            pltpu.VMEM((half, 2 * dates, lanes), f32),
        ],
        compiler_params=small,
        name="margins",
    )(place, gamma, path_counts, *gathered)
    came = lax.ppermute(out, "date", swap)
    margin = jnp.where(holder == core, out[:local_micro], came[:local_micro])
    margin = lax.dynamic_slice_in_dim(margin, core * dates, dates, 1)
    margin = jnp.swapaxes(margin, 0, 1)
    total = out[local_micro] + came[local_micro]
    step = 2
    while step < segments:
        total = total + lax.ppermute(total, "date", [(i, i ^ step) for i in range(segments)])
        step *= 2
    return (margin, total[0, 0])


def solution(mesh):
    in_specs = (
        P("date", "bucket", None, None),
        P("date", "bucket", None, None, None),
        P("date"),
        P("bucket", None, None),
        P("bucket", None),
        P("bucket", None, None),
        P(),
        P("date", "bucket", None),
        P(),
    )
    out_specs = (P("date", "bucket", None), P())


    return jax.shard_map(shards, mesh=mesh, in_specs=in_specs, out_specs=out_specs, check_vma=False)
```

```python
import functools

import jax
import jax.numpy as jnp
from jax import lax
from jax.experimental import pallas as pl
from jax.experimental.pallas import tpu as pltpu
from jax.sharding import PartitionSpec as P


epsilon = 1e-06
f32 = jnp.float32
bf16 = jnp.bfloat16
pair = 2
flight = 4
lag = 2
early = 2


def dot(a, b):
    return jnp.dot(a, b, preferred_element_type=f32)


def split(x):
    high = x.astype(bf16)
    return high, (x - high.astype(f32)).astype(bf16)


def cost(flops, read):
    return pl.CostEstimate(flops=flops, bytes_accessed=read, transcendentals=0)


def after(x, y):
    return lax.optimization_barrier((x, y))[0]


def operator_kernel(dates, buckets, a_hbm, r_hbm, w_ref, a_ref, r_ref, a_sem, r_sem):
    features = a_hbm.shape[-1]
    sens = r_hbm.shape[1]
    fetch_r = pltpu.make_async_copy(r_hbm, r_ref, r_sem)
    fetch = [
        [pltpu.make_async_copy(a_hbm.at[t, b], a_ref.at[t, b], a_sem.at[t, b]) for b in range(buckets)]
        for t in range(dates)
    ]
    for t in range(dates):
        for b in range(buckets):
            fetch[t][b].start()
        if t == 0:
            fetch_r.start()
    products = [None] * buckets
    fetch_r.wait()
    for t in range(dates):
        for b in range(buckets):
            fetch[t][b].wait()
            if t:
                products[b] = dot(a_ref[t, b], products[b]).astype(bf16)
            else:
                products[b] = a_ref[t, b]
            row = features + t * sens
            w_ref[b, row : row + sens, :] = dot(r_ref[b], products[b]).astype(bf16)
    for b in range(buckets):
        w_ref[b, :features, :] = products[b]


def local_kernel(
    dates,
    b,
    scale_ref,
    octet_ref,
    x_hbm,
    a_hbm,
    r_hbm,
    out_ref,
    x_ref,
    a_ref,
    r_ref,
    rows_ref,
    state_ref,
    x_sem,
    a_sem,
    r_sem,
):
    features, micro, lanes = x_ref.shape[1:]
    sens = r_hbm.shape[1]
    width = pair * lanes
    pieces = micro // pair
    begin = pl.multiple_of(octet_ref[0] * micro, micro)

    def fetch_x(t):
        return pltpu.make_async_copy(
            x_hbm.at[t, b, :, pl.ds(begin, micro), :], x_ref.at[t], x_sem.at[t]
        )

    def fetch_a(t):
        return pltpu.make_async_copy(a_hbm.at[t, b], a_ref.at[t], a_sem.at[t])

    fetch_r = pltpu.make_async_copy(r_hbm.at[b], r_ref, r_sem)
    for t in range(dates):
        fetch_x(t).start()
        if t:
            fetch_a(t).start()
        else:
            fetch_r.start()

    def one_date(t, first):
        fetch_x(t).wait()
        rows_ref[...] = x_ref[t].astype(f32).reshape(features * micro, lanes)
        if first:
            fetch_r.wait()
        else:
            fetch_a(t).wait()
        row = pl.multiple_of(features + t * sens, sens)
        for q in range(pieces):
            cols = slice(q * width, (q + 1) * width)
            total = scale_ref[t] * jnp.concatenate(
                [rows_ref[pl.ds(q * pair + i, features, stride=micro), :] for i in range(pair)],
                axis=1,
            )
            if not first:
                total = total + dot(a_ref[t], state_ref[:, cols])
            state = total.astype(bf16)
            state_ref[:, cols] = state
            out_ref[q, pl.ds(row, sens), :] = dot(r_ref[...], state).astype(bf16)

    one_date(0, True)

    def body(t, carry):
        one_date(t, False)
        return carry

    lax.fori_loop(1, dates, body, 0)
    for q in range(pieces):
        out_ref[q, :features, :] = state_ref[:, q * width : (q + 1) * width]


def join_operator_kernel(core_ref, mine_ref, other_ref, p_ref, q_ref, late_ref):
    features = mine_ref.shape[2]
    first = core_ref[0] == 0
    mine, other = mine_ref[0], other_ref[0]
    early = jnp.where(first, mine, other)
    late = jnp.where(first, other, mine)
    joined = dot(late, early[:features]).astype(bf16)
    p_ref[0] = joined[:features]
    seen = late.shape[0] - features
    q_ref[0, :seen, :] = early[features:]
    q_ref[0, seen:, :] = joined[features:]
    late_ref[0] = late


def join_state_kernel(b, core_ref, mine_ref, other_ref, late_ref, seen_ref, *end_refs):
    features = late_ref.shape[2]
    first = core_ref[0] == 0
    late_operator = late_ref[b]
    for q, end_ref in enumerate(end_refs):
        mine, other = mine_ref[q], other_ref[q]
        early = jnp.where(first, mine, other)
        late = jnp.where(first, other, mine)
        joined = dot(late_operator, early[:features]) + late.astype(f32)
        seen = late.shape[0] - features
        seen_ref[q, :seen, :] = early[features:].astype(f32)
        seen_ref[q, seen:, :] = joined[features:]
        end_ref[...] = joined[:features].astype(bf16)


def stage_kernel(b, up_ref, mine_ref, other_ref, a_ref, out_ref):
    up = up_ref[0] == 1
    mine, other = mine_ref[...], other_ref[...]
    early = jnp.where(up, other, mine)
    late = jnp.where(up, mine, other)
    out_ref[...] = (dot(a_ref[b], early) + late.astype(f32)).astype(bf16)


def final_kernel(
    b, q, dates, up_ref, first_ref, last_ref, phi_ref, q_ref, seen_ref, rw_ref, c_ref, out_ref
):
    sens = rw_ref.shape[1]
    width = first_ref.shape[1]
    first = first_ref[...].astype(f32)
    first = jnp.where(up_ref[0] == 1, first, jnp.zeros_like(first))
    entering = (first + dot(phi_ref[b], last_ref[...])).astype(bf16)
    seen = seen_ref[q] + dot(q_ref[b], entering)
    weight = rw_ref[b]
    ws = jnp.concatenate(
        [weight * seen[t * sens : (t + 1) * sens] for t in range(dates)], axis=1
    )
    c_high, c_low = split(c_ref[b])
    w_high, w_low = split(ws)
    mixed = dot(
        jnp.concatenate([c_high, c_low, c_high], axis=1),
        jnp.concatenate([w_high, w_high, w_low], axis=0),
    )
    within = jnp.sum(ws * mixed, axis=0, keepdims=True) + epsilon
    root = jnp.sqrt(within)
    net = jnp.clip(jnp.sum(ws, axis=0, keepdims=True), -root, root)
    for t in range(dates):
        out_ref[0, t : t + 1, :] = within[:, t * width : (t + 1) * width]
        out_ref[1, t : t + 1, :] = net[:, t * width : (t + 1) * width]


def pack_kernel(buckets, pieces, *refs):
    stats, discount_ref, out_ref = refs[:-2], refs[-2], refs[-1]
    dates = stats[0].shape[1]
    lanes = out_ref.shape[1]
    block = pair * dates
    for q in range(pieces):
        own = [stats[b * pieces + q] for b in range(buckets)]
        within = sum(ref[0] for ref in own)
        for r, value in enumerate([within] + [ref[1] for ref in own]):
            rows = jnp.concatenate(
                [value[:, i * lanes : (i + 1) * lanes] for i in range(pair)], axis=0
            )
            row = (r * pieces + q) * block
            out_ref[row : row + block, :] = rows.astype(bf16)
    out_ref[(buckets + 1) * pieces * block :, :] = discount_ref[...]


def margin_kernel(
    buckets, dates, local_micro, half, place_ref, gamma_ref, count_ref, *refs
):
    messages, (out_ref, spread_ref, margin_ref) = refs[:-3], refs[-3:]
    zs = len(messages)
    lanes = out_ref.shape[2]
    body = half * dates
    shard, core = place_ref[0], place_ref[1]
    origin = [lax.rem(shard - k + zs, zs) for k in range(zs)]
    within = 0.0
    nets = []
    for k, ref in enumerate(messages):
        within = within + ref[:body, :].astype(f32)
        for b in range(buckets):
            row = (b + 1) * body
            nets.append((origin[k] * buckets + b, ref[row : row + body, :].astype(f32)))
        row = (buckets + 1) * body
        size = local_micro * dates
        rest = ref[row : row + 2 * size, :].astype(f32)
        spread_ref[pl.ds(origin[k] * local_micro, local_micro)] = (
            rest[:size] + rest[size:]
        ).reshape(local_micro, dates, lanes)
    squares = within
    for i, (at, net) in enumerate(nets):
        coupled = 0.0
        for k, (other_at, other) in enumerate(nets):
            if k != i:
                coupled = coupled + gamma_ref[at, other_at] * other
        squares = squares + net * coupled
    root = jnp.sqrt(squares).reshape(half, dates, lanes)
    lane = lax.broadcasted_iota(jnp.int32, (dates, lanes), 1)
    total = jnp.zeros((dates, lanes), f32)
    for m in range(half):
        live = count_ref[core * half + m]
        margin = jnp.where(lane < live, root[m], f32(0.0))
        margin_ref[m] = margin
        total = total + spread_ref[core * half + m] * margin / live.astype(f32)
    total = jnp.sum(jnp.sum(total, axis=0, keepdims=True), axis=1, keepdims=True)
    out_ref[:local_micro] = margin_ref[pl.ds(place_ref[2], local_micro)]
    out_ref[local_micro] = jnp.broadcast_to(total, (dates, lanes))


def shards(
    transition,
    shocks,
    step_days,
    readout,
    risk_weight,
    correlation,
    cross_gamma,
    discount,
    path_counts,
):
    position = lax.axis_index("date")
    segments = lax.axis_size("date")
    zs = lax.axis_size("bucket")
    z = lax.axis_index("bucket")
    dates, buckets, features, batches, lanes = shocks.shape
    sens = readout.shape[1]
    scales = jnp.sqrt(step_days.astype(f32) / 30.0)
    half = batches // 2
    pieces = half // pair
    width = pair * lanes
    seen_rows = dates * sens
    rows = features + seen_rows
    core = lax.rem(position, 2)
    core_flag = core.astype(jnp.int32).reshape(1)
    stages = (segments // 2).bit_length() - 1
    ups = [lax.rem(position // (2 << s), 2).astype(jnp.int32).reshape(1) for s in range(stages)]
    swap = [(i, i ^ 1) for i in range(segments)]
    smem = pl.BlockSpec(memory_space=pltpu.SMEM)

    vmem = pl.BlockSpec(memory_space=pltpu.VMEM)
    hbm = pl.BlockSpec(memory_space=pltpu.HBM)
    small = pltpu.CompilerParams(vmem_limit_bytes=16 * 2**20)
    operators = pl.pallas_call(
        functools.partial(operator_kernel, dates, buckets),
        out_shape=jax.ShapeDtypeStruct((buckets, rows, features), bf16),
        in_specs=[hbm, hbm],
        out_specs=vmem,
        scratch_shapes=[
            pltpu.VMEM((dates, buckets, features, features), bf16),
            pltpu.VMEM((buckets, sens, features), bf16),
            pltpu.SemaphoreType.DMA((dates, buckets)),
            pltpu.SemaphoreType.DMA,
        ],
        compiler_params=small,
        cost_estimate=cost(2 * buckets * dates * features**3, 2**23),
        name="operators",
    )(transition, readout)

    def local(b, octet, scales):
        return pl.pallas_call(
            functools.partial(local_kernel, dates, b),
            out_shape=jax.ShapeDtypeStruct((pieces, rows, width), bf16),
            in_specs=[smem, smem, hbm, hbm, hbm],
            out_specs=vmem,
            scratch_shapes=[
                pltpu.VMEM((dates, features, half, lanes), bf16),
                pltpu.VMEM((dates, features, features), bf16),
                pltpu.VMEM((sens, features), bf16),
                pltpu.VMEM((features * half, lanes), f32),
                pltpu.VMEM((features, half * lanes), bf16),
                pltpu.SemaphoreType.DMA((dates,)),
                pltpu.SemaphoreType.DMA((dates,)),
                pltpu.SemaphoreType.DMA,
            ],
            compiler_params=small,
            cost_estimate=cost(2 * dates * rows * features * half * lanes // 2, 2**23),
            name="local",
        )(scales, octet, shocks, transition, readout)

    scales = after(scales, operators)
    operators_other = lax.ppermute(operators, "date", swap)
    discount = (step_days.astype(f32) / 365.0)[:, None, None] * discount
    discount_other = lax.ppermute(discount, "date", swap)
    sent = local(0, 1 - core_flag, scales)
    operators_other = after(operators_other, sent)
    late_half = lax.ppermute(sent, "date", swap)

    block3 = lambda r: pl.BlockSpec((1, r, features), lambda b: (b, 0, 0))
    block, seer, late = pl.pallas_call(
        join_operator_kernel,
        out_shape=(
            jax.ShapeDtypeStruct((buckets, features, features), bf16),
            jax.ShapeDtypeStruct((buckets, 2 * seen_rows, features), bf16),
            jax.ShapeDtypeStruct((buckets, rows, features), bf16),
        ),
        grid=(buckets,),
        in_specs=[smem, block3(rows), block3(rows)],
        out_specs=(block3(features), block3(2 * seen_rows), block3(rows)),
        cost_estimate=cost(2 * buckets * rows * features**2, 2**22),
        compiler_params=pltpu.CompilerParams(vmem_limit_bytes=16 * 2**20),
        name="join_operators",
    )(core_flag, operators, operators_other)

    combiners = []
    eye = jnp.broadcast_to(jnp.eye(features, dtype=bf16), (buckets, features, features))
    prefix = eye
    prefixes = [eye]
    for s in range(stages - 1):
        far = [(i, i ^ (2 << s)) for i in range(segments)]
        rows_half = features // 2
        part = lax.dynamic_slice_in_dim(block, core * rows_half, rows_half, 1)
        if s == 0:
            scales = after(scales, part)
        part = lax.ppermute(part, "date", far)
        if s == 0:
            own = local(0, core_flag, scales)
            part = after(part, own)
        part_other = lax.ppermute(part, "date", swap)
        first = core == 0
        other = jnp.concatenate(
            [jnp.where(first, part, part_other), jnp.where(first, part_other, part)], axis=1
        )
        up = ups[s][0] == 1
        combiners.append(jnp.where(up, block, other))
        if s == 0:
            prefix = jnp.where(up, other, eye)
        else:
            moved = jnp.einsum("bij,bjk->bik", prefix, other, preferred_element_type=f32)
            prefix = jnp.where(up, moved.astype(bf16), prefix)
        prefixes.append(prefix)
        if s < stages - 2:
            above = jnp.where(up, block, other)
            below = jnp.where(up, other, block)
            block = jnp.einsum(
                "bij,bjk->bik", above, below, preferred_element_type=f32
            ).astype(bf16)

    if stages < 2:
        own = local(0, core_flag, scales)

    ends = []
    seens = []

    def join_states(b, own, late_half):
        result = pl.pallas_call(
            functools.partial(join_state_kernel, b),
            out_shape=(jax.ShapeDtypeStruct((pieces, 2 * seen_rows, width), f32),)
            + (jax.ShapeDtypeStruct((features, width), bf16),) * pieces,
            in_specs=[smem, vmem, vmem, vmem],
            out_specs=(vmem,) * (pieces + 1),
            compiler_params=small,
            cost_estimate=cost(2 * rows * features * half * lanes, 2**22),
            name="join_states",
        )(core_flag, own, late_half, late)
        seens.append(result[0])
        ends.extend(result[1:])

    weight_column = risk_weight[:, :, None]
    count = buckets * pieces

    def stage(j, up, mine, other, combiner):
        return pl.pallas_call(
            functools.partial(stage_kernel, j // pieces),
            out_shape=jax.ShapeDtypeStruct((features, width), bf16),
            in_specs=[smem, vmem, vmem, vmem],
            out_specs=vmem,
            compiler_params=small,
            cost_estimate=cost(2 * features**2 * width, 2**20),
            name="stage",
        )(up, mine, other, combiner)

    def final(j, up, first, last, operator):
        b, q = divmod(j, pieces)
        return pl.pallas_call(
            functools.partial(final_kernel, b, q, 2 * dates),
            out_shape=jax.ShapeDtypeStruct((2, 2 * dates, width), f32),
            in_specs=[smem] + [vmem] * 7,
            out_specs=vmem,
            compiler_params=small,
            cost_estimate=cost(4 * features**2 * width, 2**21),
            name="final",
        )(up, first, last, operator, seer, seens[b], weight_column, correlation)

    arrived = [[] for _ in range(stages)]
    leaving = [[] for _ in range(stages)]
    holds = {}
    results = []

    def held(s, j):
        if s == 0:
            return jnp.zeros((features, width), bf16), jnp.ones((1,), jnp.int32)
        if s == 1:
            return arrived[0][j], ups[0]
        if (s, j) not in holds:
            before, flag = held(s - 1, j)
            before = jnp.where(flag[0] == 1, before, jnp.zeros_like(before)).astype(f32)
            moved = dot(prefixes[s - 1][j // pieces], arrived[s - 1][j])
            value = jnp.where(ups[s - 1][0] == 1, before + moved, before)
            holds[s, j] = value.astype(bf16)
        return holds[s, j], jnp.ones((1,), jnp.int32)

    def advance(s, behind=None):
        j = len(arrived[s])
        last = s == stages - 1
        bit = 2 << s
        link = [(i, i ^ bit) for i in range(segments) if not (last and i & bit)]
        if s == 0:
            out = ends[j]
        else:
            near = arrived[s - 1][j]
            if behind is not None:
                near = after(near, results[behind])
            out = stage(j, ups[s - 1], leaving[s - 1][j], near, combiners[s - 1])
        if j >= flight:
            out = after(out, arrived[s][j - flight])
        leaving[s].append(out)
        arrived[s].append(lax.ppermute(out, "date", link))

    def finish():
        i = len(results)
        before, flag = held(stages - 1, i)
        results.append(final(i, flag, before, arrived[-1][i], prefixes[stages - 1]))

    join_states(0, own, late_half)
    for b in range(buckets):
        for _ in range(pieces):
            advance(0)
        if b + 1 < buckets:
            scales = after(scales, ends[-1])
            sent = local(b + 1, 1 - core_flag, scales)
            late_half = lax.ppermute(sent, "date", swap)
            if stages > 1:
                for _ in range(early):
                    at = len(arrived[1])
                    arrived[0][at] = after(arrived[0][at], sent)
                    advance(1)
                    scales = after(scales, leaving[1][-1])
            else:
                scales = after(scales, sent)
            own = local(b + 1, core_flag, scales)
            join_states(b + 1, own, late_half)
    for s in range(1, stages):
        last = s == stages - 1
        while len(arrived[s]) < count:
            j = len(arrived[s])
            while last and len(results) < j - lag:
                finish()
            advance(s, j - lag - 1 if last and j > lag else None)
    while len(results) < count:
        finish()

    local_micro = discount.shape[1]
    both = jnp.where(
        core == 0,
        jnp.stack([discount, discount_other]),
        jnp.stack([discount_other, discount]),
    ).reshape(2 * dates, local_micro, lanes)
    high, low = split(jnp.swapaxes(both, 0, 1))
    carried = jnp.concatenate([high.reshape(-1, lanes), low.reshape(-1, lanes)], axis=0)
    body_rows = (buckets + 1) * half * 2 * dates
    message = pl.pallas_call(
        functools.partial(pack_kernel, buckets, pieces),
        out_shape=jax.ShapeDtypeStruct((body_rows + carried.shape[0], lanes), bf16),
        in_specs=[vmem] * (count + 1),
        out_specs=vmem,
        compiler_params=small,
        name="pack",
    )(*results, carried)
    gathered = [message]
    for k in range(1, zs):
        gathered.append(lax.ppermute(message, "bucket", [(i, (i + k) % zs) for i in range(zs)]))
    gamma = (
        0.5
        * (cross_gamma + cross_gamma.T)
        * (1.0 - jnp.eye(cross_gamma.shape[0], dtype=f32))
    )
    start = z * local_micro
    holder = start // half
    place = jnp.stack([z, core, start - holder * half]).astype(jnp.int32)
    out = pl.pallas_call(
        functools.partial(margin_kernel, buckets, 2 * dates, local_micro, half),
        out_shape=jax.ShapeDtypeStruct((local_micro + 1, 2 * dates, lanes), f32),
        in_specs=[smem] * 3 + [vmem] * zs,
        out_specs=vmem,
        scratch_shapes=[
            pltpu.VMEM((batches, 2 * dates, lanes), f32),
            pltpu.VMEM((half, 2 * dates, lanes), f32),
        ],
        compiler_params=small,
        name="margins",
    )(place, gamma, path_counts, *gathered)
    came = lax.ppermute(out, "date", swap)
    margin = jnp.where(holder == core, out[:local_micro], came[:local_micro])
    margin = lax.dynamic_slice_in_dim(margin, core * dates, dates, 1)
    margin = jnp.swapaxes(margin, 0, 1)
    total = out[local_micro] + came[local_micro]
    step = 2
    while step < segments:
        total = total + lax.ppermute(total, "date", [(i, i ^ step) for i in range(segments)])
        step *= 2
    return (margin, total[0, 0])


def solution(mesh):
    in_specs = (
        P("date", "bucket", None, None),
        P("date", "bucket", None, None, None),
        P("date"),
        P("bucket", None, None),
        P("bucket", None),
        P("bucket", None, None),
        P(),
        P("date", "bucket", None),
        P(),
    )
    out_specs = (P("date", "bucket", None), P())


    return jax.shard_map(shards, mesh=mesh, in_specs=in_specs, out_specs=out_specs, check_vma=False)
```

```python
import functools

import jax
import jax.numpy as jnp
from jax import lax
from jax.experimental import pallas as pl
from jax.experimental.pallas import tpu as pltpu
from jax.sharding import PartitionSpec as P


epsilon = 1e-06
f32 = jnp.float32
bf16 = jnp.bfloat16
pair = 4
flight = 2
lag = 1
early = 1


def dot(a, b):
    return jnp.dot(a, b, preferred_element_type=f32)


def split(x):
    high = x.astype(bf16)
    return high, (x - high.astype(f32)).astype(bf16)


def cost(flops, read):
    return pl.CostEstimate(flops=flops, bytes_accessed=read, transcendentals=0)


def after(x, y):
    return lax.optimization_barrier((x, y))[0]


def operator_kernel(dates, a_ref, r_ref, w_ref):
    features = a_ref.shape[-1]
    sens = r_ref.shape[1]
    product = a_ref[0, 0]
    for t in range(dates):
        if t:
            product = dot(a_ref[t, 0], product).astype(bf16)
        row = features + t * sens
        w_ref[0, row : row + sens, :] = dot(r_ref[0], product).astype(bf16)
    w_ref[0, :features, :] = product


def local_kernel(
    dates,
    b,
    scale_ref,
    octet_ref,
    x_hbm,
    a_hbm,
    r_hbm,
    out_ref,
    x_ref,
    a_ref,
    r_ref,
    rows_ref,
    state_ref,
    x_sem,
    a_sem,
    r_sem,
):
    features, micro, lanes = x_ref.shape[1:]
    sens = r_hbm.shape[1]
    width = pair * lanes
    pieces = micro // pair
    begin = pl.multiple_of(octet_ref[0] * micro, micro)

    def fetch_x(t):
        return pltpu.make_async_copy(
            x_hbm.at[t, b, :, pl.ds(begin, micro), :], x_ref.at[t], x_sem.at[t]
        )

    def fetch_a(t):
        return pltpu.make_async_copy(a_hbm.at[t, b], a_ref.at[t], a_sem.at[t])

    fetch_r = pltpu.make_async_copy(r_hbm.at[b], r_ref, r_sem)
    for t in range(dates):
        fetch_x(t).start()
        if t:
            fetch_a(t).start()
        else:
            fetch_r.start()
    for t in range(dates):
        fetch_x(t).wait()
        rows_ref[...] = x_ref[t].astype(f32).reshape(features * micro, lanes)
        if t:
            fetch_a(t).wait()
        else:
            fetch_r.wait()
        for q in range(pieces):
            cols = slice(q * width, (q + 1) * width)
            total = scale_ref[t] * jnp.concatenate(
                [rows_ref[pl.ds(q * pair + i, features, stride=micro), :] for i in range(pair)],
                axis=1,
            )
            if t:
                total = total + dot(a_ref[t], state_ref[:, cols])
            state_ref[:, cols] = total.astype(bf16)
        row = features + t * sens
        for q in range(pieces):
            state = state_ref[:, q * width : (q + 1) * width]
            out_ref[q, row : row + sens, :] = dot(r_ref[...], state).astype(bf16)
    for q in range(pieces):
        out_ref[q, :features, :] = state_ref[:, q * width : (q + 1) * width]


def join_operator_kernel(core_ref, mine_ref, other_ref, p_ref, q_ref, late_ref):
    features = mine_ref.shape[2]
    first = core_ref[0] == 0
    mine, other = mine_ref[0], other_ref[0]
    early = jnp.where(first, mine, other)
    late = jnp.where(first, other, mine)
    joined = dot(late, early[:features]).astype(bf16)
    p_ref[0] = joined[:features]
    seen = late.shape[0] - features
    q_ref[0, :seen, :] = early[features:]
    q_ref[0, seen:, :] = joined[features:]
    late_ref[0] = late


def join_state_kernel(b, core_ref, mine_ref, other_ref, late_ref, seen_ref, *end_refs):
    features = late_ref.shape[2]
    first = core_ref[0] == 0
    late_operator = late_ref[b]
    for q, end_ref in enumerate(end_refs):
        mine, other = mine_ref[q], other_ref[q]
        early = jnp.where(first, mine, other)
        late = jnp.where(first, other, mine)
        joined = dot(late_operator, early[:features]) + late.astype(f32)
        seen = late.shape[0] - features
        seen_ref[q, :seen, :] = early[features:].astype(f32)
        seen_ref[q, seen:, :] = joined[features:]
        end_ref[...] = joined[:features].astype(bf16)


def stage_kernel(b, up_ref, mine_ref, other_ref, a_ref, out_ref):
    up = up_ref[0] == 1
    mine, other = mine_ref[...], other_ref[...]
    early = jnp.where(up, other, mine)
    late = jnp.where(up, mine, other)
    out_ref[...] = (dot(a_ref[b], early) + late.astype(f32)).astype(bf16)


def final_kernel(
    b, q, dates, up_ref, first_ref, last_ref, phi_ref, q_ref, seen_ref, rw_ref, c_ref, out_ref
):
    sens = rw_ref.shape[1]
    width = first_ref.shape[1]
    first = first_ref[...].astype(f32)
    first = jnp.where(up_ref[0] == 1, first, jnp.zeros_like(first))
    entering = (first + dot(phi_ref[b], last_ref[...])).astype(bf16)
    seen = seen_ref[q] + dot(q_ref[b], entering)
    weight = rw_ref[b]
    ws = jnp.concatenate(
        [weight * seen[t * sens : (t + 1) * sens] for t in range(dates)], axis=1
    )
    c_high, c_low = split(c_ref[b])
    w_high, w_low = split(ws)
    mixed = dot(
        jnp.concatenate([c_high, c_low, c_high], axis=1),
        jnp.concatenate([w_high, w_high, w_low], axis=0),
    )
    within = jnp.sum(ws * mixed, axis=0, keepdims=True) + epsilon
    root = jnp.sqrt(within)
    net = jnp.clip(jnp.sum(ws, axis=0, keepdims=True), -root, root)
    for t in range(dates):
        out_ref[0, t : t + 1, :] = within[:, t * width : (t + 1) * width]
        out_ref[1, t : t + 1, :] = net[:, t * width : (t + 1) * width]


def pack_kernel(buckets, pieces, *refs):
    stats, discount_ref, out_ref = refs[:-2], refs[-2], refs[-1]
    dates = stats[0].shape[1]
    lanes = out_ref.shape[1]
    block = pair * dates
    for q in range(pieces):
        own = [stats[b * pieces + q] for b in range(buckets)]
        within = sum(ref[0] for ref in own)
        for r, value in enumerate([within] + [ref[1] for ref in own]):
            rows = jnp.concatenate(
                [value[:, i * lanes : (i + 1) * lanes] for i in range(pair)], axis=0
            )
            row = (r * pieces + q) * block
            out_ref[row : row + block, :] = rows.astype(bf16)
    out_ref[(buckets + 1) * pieces * block :, :] = discount_ref[...]


def margin_kernel(
    buckets, dates, local_micro, half, place_ref, gamma_ref, count_ref, *refs
):
    messages, (out_ref, spread_ref, margin_ref) = refs[:-3], refs[-3:]
    zs = len(messages)
    lanes = out_ref.shape[2]
    body = half * dates
    shard, core = place_ref[0], place_ref[1]
    origin = [lax.rem(shard - k + zs, zs) for k in range(zs)]
    within = 0.0
    nets = []
    for k, ref in enumerate(messages):
        within = within + ref[:body, :].astype(f32)
        for b in range(buckets):
            row = (b + 1) * body
            nets.append((origin[k] * buckets + b, ref[row : row + body, :].astype(f32)))
        row = (buckets + 1) * body
        size = local_micro * dates
        rest = ref[row : row + 2 * size, :].astype(f32)
        spread_ref[pl.ds(origin[k] * local_micro, local_micro)] = (
            rest[:size] + rest[size:]
        ).reshape(local_micro, dates, lanes)
    squares = within
    for i, (at, net) in enumerate(nets):
        coupled = 0.0
        for k, (other_at, other) in enumerate(nets):
            if k != i:
                coupled = coupled + gamma_ref[at, other_at] * other
        squares = squares + net * coupled
    root = jnp.sqrt(squares).reshape(half, dates, lanes)
    lane = lax.broadcasted_iota(jnp.int32, (dates, lanes), 1)
    total = jnp.zeros((dates, lanes), f32)
    for m in range(half):
        live = count_ref[core * half + m]
        margin = jnp.where(lane < live, root[m], f32(0.0))
        margin_ref[m] = margin
        total = total + spread_ref[core * half + m] * margin / live.astype(f32)
    total = jnp.sum(jnp.sum(total, axis=0, keepdims=True), axis=1, keepdims=True)
    out_ref[:local_micro] = margin_ref[pl.ds(place_ref[2], local_micro)]
    out_ref[local_micro] = jnp.broadcast_to(total, (dates, lanes))


def shards(
    transition,
    shocks,
    step_days,
    readout,
    risk_weight,
    correlation,
    cross_gamma,
    discount,
    path_counts,
):
    position = lax.axis_index("date")
    segments = lax.axis_size("date")
    zs = lax.axis_size("bucket")
    z = lax.axis_index("bucket")
    dates, buckets, features, batches, lanes = shocks.shape
    sens = readout.shape[1]
    scales = jnp.sqrt(step_days.astype(f32) / 30.0)
    half = batches // 2
    pieces = half // pair
    width = pair * lanes
    seen_rows = dates * sens
    rows = features + seen_rows
    core = lax.rem(position, 2)
    core_flag = core.astype(jnp.int32).reshape(1)
    stages = (segments // 2).bit_length() - 1
    ups = [lax.rem(position // (2 << s), 2).astype(jnp.int32).reshape(1) for s in range(stages)]
    swap = [(i, i ^ 1) for i in range(segments)]
    smem = pl.BlockSpec(memory_space=pltpu.SMEM)

    vmem = pl.BlockSpec(memory_space=pltpu.VMEM)
    hbm = pl.BlockSpec(memory_space=pltpu.HBM)
    small = pltpu.CompilerParams(vmem_limit_bytes=16 * 2**20)
    large = pltpu.CompilerParams(vmem_limit_bytes=50 * 2**20)
    operators = pl.pallas_call(
        functools.partial(operator_kernel, dates),
        out_shape=jax.ShapeDtypeStruct((buckets, rows, features), bf16),
        grid=(buckets,),
        in_specs=[
            pl.BlockSpec((dates, 1, features, features), lambda b: (0, b, 0, 0)),
            pl.BlockSpec((1, sens, features), lambda b: (b, 0, 0)),
        ],
        out_specs=pl.BlockSpec((1, rows, features), lambda b: (b, 0, 0)),
        cost_estimate=cost(2 * buckets * dates * features**3, 2**23),
        compiler_params=pltpu.CompilerParams(vmem_limit_bytes=50 * 2**20),
        name="operators",
    )(transition, readout)

    def local(b, octet, scales):
        return pl.pallas_call(
            functools.partial(local_kernel, dates, b),
            out_shape=jax.ShapeDtypeStruct((pieces, rows, width), bf16),
            in_specs=[smem, smem, hbm, hbm, hbm],
            out_specs=vmem,
            scratch_shapes=[
                pltpu.VMEM((dates, features, half, lanes), bf16),
                pltpu.VMEM((dates, features, features), bf16),
                pltpu.VMEM((sens, features), bf16),
                pltpu.VMEM((features * half, lanes), f32),
                pltpu.VMEM((features, half * lanes), bf16),
                pltpu.SemaphoreType.DMA((dates,)),
                pltpu.SemaphoreType.DMA((dates,)),
                pltpu.SemaphoreType.DMA,
            ],
            compiler_params=large,
            cost_estimate=cost(2 * dates * rows * features * half * lanes // 2, 2**23),
            name="local",
        )(scales, octet, shocks, transition, readout)

    scales = after(scales, operators)
    operators_other = lax.ppermute(operators, "date", swap)
    discount = (step_days.astype(f32) / 365.0)[:, None, None] * discount
    discount_other = lax.ppermute(discount, "date", swap)
    sent = local(0, 1 - core_flag, scales)
    operators_other = after(operators_other, sent)
    late_half = lax.ppermute(sent, "date", swap)

    block3 = lambda r: pl.BlockSpec((1, r, features), lambda b: (b, 0, 0))
    block, seer, late = pl.pallas_call(
        join_operator_kernel,
        out_shape=(
            jax.ShapeDtypeStruct((buckets, features, features), bf16),
            jax.ShapeDtypeStruct((buckets, 2 * seen_rows, features), bf16),
            jax.ShapeDtypeStruct((buckets, rows, features), bf16),
        ),
        grid=(buckets,),
        in_specs=[smem, block3(rows), block3(rows)],
        out_specs=(block3(features), block3(2 * seen_rows), block3(rows)),
        cost_estimate=cost(2 * buckets * rows * features**2, 2**22),
        compiler_params=pltpu.CompilerParams(vmem_limit_bytes=16 * 2**20),
        name="join_operators",
    )(core_flag, operators, operators_other)

    combiners = []
    eye = jnp.broadcast_to(jnp.eye(features, dtype=bf16), (buckets, features, features))
    prefix = eye
    prefixes = [eye]
    for s in range(stages - 1):
        far = [(i, i ^ (2 << s)) for i in range(segments)]
        rows_half = features // 2
        part = lax.dynamic_slice_in_dim(block, core * rows_half, rows_half, 1)
        if s == 0:
            scales = after(scales, part)
        part = lax.ppermute(part, "date", far)
        if s == 0:
            own = local(0, core_flag, scales)
            part = after(part, own)
        part_other = lax.ppermute(part, "date", swap)
        first = core == 0
        other = jnp.concatenate(
            [jnp.where(first, part, part_other), jnp.where(first, part_other, part)], axis=1
        )
        up = ups[s][0] == 1
        combiners.append(jnp.where(up, block, other))
        if s == 0:
            prefix = jnp.where(up, other, eye)
        else:
            moved = jnp.einsum("bij,bjk->bik", prefix, other, preferred_element_type=f32)
            prefix = jnp.where(up, moved.astype(bf16), prefix)
        prefixes.append(prefix)
        if s < stages - 2:
            above = jnp.where(up, block, other)
            below = jnp.where(up, other, block)
            block = jnp.einsum(
                "bij,bjk->bik", above, below, preferred_element_type=f32
            ).astype(bf16)

    if stages < 2:
        own = local(0, core_flag, scales)

    ends = []
    seens = []

    def join_states(b, own, late_half):
        result = pl.pallas_call(
            functools.partial(join_state_kernel, b),
            out_shape=(jax.ShapeDtypeStruct((pieces, 2 * seen_rows, width), f32),)
            + (jax.ShapeDtypeStruct((features, width), bf16),) * pieces,
            in_specs=[smem, vmem, vmem, vmem],
            out_specs=(vmem,) * (pieces + 1),
            compiler_params=small,
            cost_estimate=cost(2 * rows * features * half * lanes, 2**22),
            name="join_states",
        )(core_flag, own, late_half, late)
        seens.append(result[0])
        ends.extend(result[1:])

    weight_column = risk_weight[:, :, None]
    count = buckets * pieces

    def stage(j, up, mine, other, combiner):
        return pl.pallas_call(
            functools.partial(stage_kernel, j // pieces),
            out_shape=jax.ShapeDtypeStruct((features, width), bf16),
            in_specs=[smem, vmem, vmem, vmem],
            out_specs=vmem,
            compiler_params=small,
            cost_estimate=cost(2 * features**2 * width, 2**20),
            name="stage",
        )(up, mine, other, combiner)

    def final(j, up, first, last, operator):
        b, q = divmod(j, pieces)
        return pl.pallas_call(
            functools.partial(final_kernel, b, q, 2 * dates),
            out_shape=jax.ShapeDtypeStruct((2, 2 * dates, width), f32),
            in_specs=[smem] + [vmem] * 7,
            out_specs=vmem,
            compiler_params=small,
            cost_estimate=cost(4 * features**2 * width, 2**21),
            name="final",
        )(up, first, last, operator, seer, seens[b], weight_column, correlation)

    arrived = [[] for _ in range(stages)]
    leaving = [[] for _ in range(stages)]
    holds = {}
    results = []

    def held(s, j):
        if s == 0:
            return jnp.zeros((features, width), bf16), jnp.ones((1,), jnp.int32)
        if s == 1:
            return arrived[0][j], ups[0]
        if (s, j) not in holds:
            before, flag = held(s - 1, j)
            before = jnp.where(flag[0] == 1, before, jnp.zeros_like(before)).astype(f32)
            moved = dot(prefixes[s - 1][j // pieces], arrived[s - 1][j])
            value = jnp.where(ups[s - 1][0] == 1, before + moved, before)
            holds[s, j] = value.astype(bf16)
        return holds[s, j], jnp.ones((1,), jnp.int32)

    def advance(s, behind=None):
        j = len(arrived[s])
        last = s == stages - 1
        bit = 2 << s
        link = [(i, i ^ bit) for i in range(segments) if not (last and i & bit)]
        if s == 0:
            out = ends[j]
        else:
            near = arrived[s - 1][j]
            if behind is not None:
                near = after(near, results[behind])
            out = stage(j, ups[s - 1], leaving[s - 1][j], near, combiners[s - 1])
        if j >= flight:
            out = after(out, arrived[s][j - flight])
        leaving[s].append(out)
        arrived[s].append(lax.ppermute(out, "date", link))

    def finish():
        i = len(results)
        before, flag = held(stages - 1, i)
        results.append(final(i, flag, before, arrived[-1][i], prefixes[stages - 1]))

    join_states(0, own, late_half)
    for b in range(buckets):
        for _ in range(pieces):
            advance(0)
        if b + 1 < buckets:
            scales = after(scales, ends[-1])
            sent = local(b + 1, 1 - core_flag, scales)
            late_half = lax.ppermute(sent, "date", swap)
            if stages > 1:
                for _ in range(early):
                    at = len(arrived[1])
                    arrived[0][at] = after(arrived[0][at], sent)
                    advance(1)
                    scales = after(scales, leaving[1][-1])
            else:
                scales = after(scales, sent)
            own = local(b + 1, core_flag, scales)
            join_states(b + 1, own, late_half)
    for s in range(1, stages):
        last = s == stages - 1
        while len(arrived[s]) < count:
            j = len(arrived[s])
            while last and len(results) < j - lag:
                finish()
            advance(s, j - lag - 1 if last and j > lag else None)
    while len(results) < count:
        finish()

    local_micro = discount.shape[1]
    both = jnp.where(
        core == 0,
        jnp.stack([discount, discount_other]),
        jnp.stack([discount_other, discount]),
    ).reshape(2 * dates, local_micro, lanes)
    high, low = split(jnp.swapaxes(both, 0, 1))
    carried = jnp.concatenate([high.reshape(-1, lanes), low.reshape(-1, lanes)], axis=0)
    body_rows = (buckets + 1) * half * 2 * dates
    message = pl.pallas_call(
        functools.partial(pack_kernel, buckets, pieces),
        out_shape=jax.ShapeDtypeStruct((body_rows + carried.shape[0], lanes), bf16),
        in_specs=[vmem] * (count + 1),
        out_specs=vmem,
        compiler_params=small,
        name="pack",
    )(*results, carried)
    gathered = [message]
    for k in range(1, zs):
        gathered.append(lax.ppermute(message, "bucket", [(i, (i + k) % zs) for i in range(zs)]))
    gamma = (
        0.5
        * (cross_gamma + cross_gamma.T)
        * (1.0 - jnp.eye(cross_gamma.shape[0], dtype=f32))
    )
    start = z * local_micro
    holder = start // half
    place = jnp.stack([z, core, start - holder * half]).astype(jnp.int32)
    out = pl.pallas_call(
        functools.partial(margin_kernel, buckets, 2 * dates, local_micro, half),
        out_shape=jax.ShapeDtypeStruct((local_micro + 1, 2 * dates, lanes), f32),
        in_specs=[smem] * 3 + [vmem] * zs,
        out_specs=vmem,
        scratch_shapes=[
            pltpu.VMEM((batches, 2 * dates, lanes), f32),
            pltpu.VMEM((half, 2 * dates, lanes), f32),
        ],
        compiler_params=small,
        name="margins",
    )(place, gamma, path_counts, *gathered)
    came = lax.ppermute(out, "date", swap)
    margin = jnp.where(holder == core, out[:local_micro], came[:local_micro])
    margin = lax.dynamic_slice_in_dim(margin, core * dates, dates, 1)
    margin = jnp.swapaxes(margin, 0, 1)
    total = out[local_micro] + came[local_micro]
    step = 2
    while step < segments:
        total = total + lax.ppermute(total, "date", [(i, i ^ step) for i in range(segments)])
        step *= 2
    return (margin, total[0, 0])


def solution(mesh):
    in_specs = (
        P("date", "bucket", None, None),
        P("date", "bucket", None, None, None),
        P("date"),
        P("bucket", None, None),
        P("bucket", None),
        P("bucket", None, None),
        P(),
        P("date", "bucket", None),
        P(),
    )
    out_specs = (P("date", "bucket", None), P())


    return jax.shard_map(shards, mesh=mesh, in_specs=in_specs, out_specs=out_specs, check_vma=False)
```

```python
import functools

import jax
import jax.numpy as jnp
from jax import lax
from jax.experimental import pallas as pl
from jax.experimental.pallas import tpu as pltpu
from jax.sharding import PartitionSpec as P


epsilon = 1e-06
f32 = jnp.float32
bf16 = jnp.bfloat16
pair = 2
flight = 8
lag = 1
early = 1


def chunks(units, bucket, buckets):
    sizes = [2] * (units // 2) + [1] * (units % 2)
    if bucket == buckets - 1 and units % 2 == 0:
        sizes[-1:] = [1, 1]
    return sizes


def dot(a, b):
    return jnp.dot(a, b, preferred_element_type=f32)


def split(x):
    high = x.astype(bf16)
    return high, (x - high.astype(f32)).astype(bf16)


def cost(flops, read):
    return pl.CostEstimate(flops=flops, bytes_accessed=read, transcendentals=0)


def after(x, y):
    return lax.optimization_barrier((x, y))[0]


def operator_kernel(dates, a_ref, r_ref, w_ref):
    features = a_ref.shape[-1]
    sens = r_ref.shape[1]
    product = a_ref[0, 0]
    for t in range(dates):
        if t:
            product = dot(a_ref[t, 0], product).astype(bf16)
        row = features + t * sens
        w_ref[0, row : row + sens, :] = dot(r_ref[0], product).astype(bf16)
    w_ref[0, :features, :] = product


def local_kernel(
    dates,
    b,
    scale_ref,
    octet_ref,
    x_hbm,
    a_hbm,
    r_hbm,
    out_ref,
    x_ref,
    a_ref,
    r_ref,
    rows_ref,
    state_ref,
    x_sem,
    a_sem,
    r_sem,
):
    features, micro, lanes = x_ref.shape[1:]
    sens = r_hbm.shape[1]
    width = pair * lanes
    pieces = micro // pair
    begin = pl.multiple_of(octet_ref[0] * micro, micro)

    def fetch_x(t):
        return pltpu.make_async_copy(
            x_hbm.at[t, b, :, pl.ds(begin, micro), :], x_ref.at[t], x_sem.at[t]
        )

    def fetch_a(t):
        return pltpu.make_async_copy(a_hbm.at[t, b], a_ref.at[t], a_sem.at[t])

    fetch_r = pltpu.make_async_copy(r_hbm.at[b], r_ref, r_sem)
    for t in range(dates):
        fetch_x(t).start()
        if t:
            fetch_a(t).start()
        else:
            fetch_r.start()
    for t in range(dates):
        fetch_x(t).wait()
        rows_ref[...] = x_ref[t].astype(f32).reshape(features * micro, lanes)
        if t:
            fetch_a(t).wait()
        else:
            fetch_r.wait()
        for q in range(pieces):
            cols = slice(q * width, (q + 1) * width)
            total = scale_ref[t] * jnp.concatenate(
                [rows_ref[pl.ds(q * pair + i, features, stride=micro), :] for i in range(pair)],
                axis=1,
            )
            if t:
                total = total + dot(a_ref[t], state_ref[:, cols])
            state_ref[:, cols] = total.astype(bf16)
        row = features + t * sens
        for q in range(pieces):
            state = state_ref[:, q * width : (q + 1) * width]
            out_ref[q, row : row + sens, :] = dot(r_ref[...], state).astype(bf16)
    for q in range(pieces):
        out_ref[q, :features, :] = state_ref[:, q * width : (q + 1) * width]


def join_operator_kernel(core_ref, mine_ref, other_ref, p_ref, q_ref, late_ref, part_ref):
    features = mine_ref.shape[2]
    first = core_ref[0] == 0
    mine, other = mine_ref[0], other_ref[0]
    early = jnp.where(first, mine, other)
    late = jnp.where(first, other, mine)
    joined = dot(late, early[:features]).astype(bf16)
    p_ref[0] = joined[:features]
    part_ref[0] = jnp.where(first, joined[: features // 2], joined[features // 2 : features])
    seen = late.shape[0] - features
    q_ref[0, :seen, :] = early[features:]
    q_ref[0, seen:, :] = joined[features:]
    late_ref[0] = late


def join_state_kernel(
    b,
    sizes,
    core_ref,
    mine_hbm,
    other_hbm,
    late_hbm,
    seen_ref,
    *refs,
):
    end_refs = refs[:-6]
    mine_ref, other_ref, late_ref, mine_sem, other_sem, late_sem = refs[-6:]
    features = late_ref.shape[1]
    width = mine_ref.shape[2]
    first = core_ref[0] == 0
    fetch = pltpu.make_async_copy(late_hbm.at[b], late_ref, late_sem)
    fetch.start()
    pieces = [
        (
            pltpu.make_async_copy(mine_hbm.at[q], mine_ref.at[q], mine_sem.at[q]),
            pltpu.make_async_copy(other_hbm.at[q], other_ref.at[q], other_sem.at[q]),
        )
        for q in range(sum(sizes))
    ]
    for one, two in pieces:
        one.start()
        two.start()
    fetch.wait()
    late_operator = late_ref[...]
    q = 0
    for end_ref, size in zip(end_refs, sizes):
        for i in range(size):
            for piece in pieces[q]:
                piece.wait()
            mine, other = mine_ref[q], other_ref[q]
            early = jnp.where(first, mine, other)
            late = jnp.where(first, other, mine)
            joined = dot(late_operator, early[:features]) + late.astype(f32)
            seen = late.shape[0] - features
            seen_ref[q, :seen, :] = early[features:]
            seen_ref[q, seen:, :] = joined[features:].astype(bf16)
            end_ref[:, i * width : (i + 1) * width] = joined[:features].astype(bf16)
            q += 1


def far_copies(b, core, part_hbm, part_other_hbm, a_ref, sem):
    half = part_hbm.shape[1]
    near = pl.ds(pl.multiple_of(core * half, half), half)
    away = pl.ds(pl.multiple_of((1 - core) * half, half), half)
    return (
        pltpu.make_async_copy(part_hbm.at[b], a_ref.at[near], sem.at[0]),
        pltpu.make_async_copy(part_other_hbm.at[b], a_ref.at[away], sem.at[1]),
    )


def first_stage_kernel(
    b, flag_ref, mine_ref, other_ref, block_hbm, part_hbm, part_other_hbm, out_ref, a_ref, sem
):
    up = flag_ref[1] == 1

    @pl.when(up)
    def _():
        copy = pltpu.make_async_copy(block_hbm.at[b], a_ref, sem.at[0])
        copy.start()
        copy.wait()

    @pl.when(flag_ref[1] == 0)
    def _():
        copies = far_copies(b, flag_ref[0], part_hbm, part_other_hbm, a_ref, sem)
        for copy in copies:
            copy.start()
        for copy in copies:
            copy.wait()

    mine, other = mine_ref[...], other_ref[...]
    early = jnp.where(up, other, mine)
    late = jnp.where(up, mine, other)
    out_ref[...] = (dot(a_ref[...], early) + late.astype(f32)).astype(bf16)


def stage_kernel(b, up_ref, mine_ref, other_ref, a_ref, out_ref):
    up = up_ref[0] == 1
    mine, other = mine_ref[...], other_ref[...]
    early = jnp.where(up, other, mine)
    late = jnp.where(up, mine, other)
    out_ref[...] = (dot(a_ref[b], early) + late.astype(f32)).astype(bf16)


def final_kernel(b, q, dates, halves, flag_ref, first_ref, last_ref, *refs):
    prefix, (q_hbm, seen_hbm, rw_ref, c_ref, out_ref) = refs[:-9], refs[-9:-4]
    a_ref, q_ref, seen_ref, sem = refs[-4:]
    sens = rw_ref.shape[1]
    width = first_ref.shape[1]
    units = seen_ref.shape[0]
    fetch_q = pltpu.make_async_copy(q_hbm.at[b], q_ref, sem.at[2])
    fetch_seen = pltpu.make_async_copy(seen_hbm.at[pl.ds(q, units)], seen_ref, sem.at[3])
    if halves:
        copies = far_copies(b, flag_ref[0], *prefix, a_ref, sem)
    else:
        copies = (pltpu.make_async_copy(prefix[0].at[b], a_ref, sem.at[0]),)
    for copy in copies:
        copy.start()
    fetch_q.start()
    fetch_seen.start()
    for copy in copies:
        copy.wait()
    up = flag_ref[1] == 1
    last = last_ref[...]
    moved = first_ref[...].astype(f32) + dot(a_ref[...], last)
    entering = jnp.where(up, moved.astype(bf16), last)
    fetch_q.wait()
    seen = dot(q_ref[...], entering)
    fetch_seen.wait()
    seen = seen + jnp.concatenate([seen_ref[i] for i in range(units)], axis=1).astype(f32)
    weight = rw_ref[b]
    ws = jnp.concatenate(
        [weight * seen[t * sens : (t + 1) * sens] for t in range(dates)], axis=1
    )
    c_high, c_low = split(c_ref[b])
    w_high, w_low = split(ws)
    mixed = dot(
        jnp.concatenate([c_high, c_low, c_high], axis=1),
        jnp.concatenate([w_high, w_high, w_low], axis=0),
    )
    within = jnp.sum(ws * mixed, axis=0, keepdims=True) + epsilon
    root = jnp.sqrt(within)
    net = jnp.clip(jnp.sum(ws, axis=0, keepdims=True), -root, root)
    for t in range(dates):
        out_ref[0, t : t + 1, :] = within[:, t * width : (t + 1) * width]
        out_ref[1, t : t + 1, :] = net[:, t * width : (t + 1) * width]


def pack_kernel(places, buckets, half, *refs):
    stats, discount_ref, out_ref = refs[:-2], refs[-2], refs[-1]
    dates = stats[0].shape[1]
    lanes = out_ref.shape[1]

    def value(kind, b, m):
        j, lane = places[b, m]
        return stats[j][kind, :, lane * lanes : (lane + 1) * lanes]

    for m in range(0, half, 2):
        block = [[value(1, b, m + i) for i in range(2)] for b in range(buckets)]
        block.insert(0, [sum(value(0, b, m + i) for b in range(buckets)) for i in range(2)])
        for r, parts in enumerate(block):
            row = (r * half + m) * dates
            out_ref[row : row + 2 * dates, :] = jnp.concatenate(parts, axis=0).astype(bf16)
    out_ref[(buckets + 1) * half * dates :, :] = discount_ref[...]


def margin_kernel(
    buckets, dates, local_micro, half, place_ref, gamma_ref, count_ref, *refs
):
    messages, (out_ref, spread_ref, margin_ref) = refs[:-3], refs[-3:]
    zs = len(messages)
    lanes = out_ref.shape[2]
    body = half * dates
    shard, core = place_ref[0], place_ref[1]
    origin = [lax.rem(shard - k + zs, zs) for k in range(zs)]
    within = 0.0
    nets = []
    for k, ref in enumerate(messages):
        within = within + ref[:body, :].astype(f32)
        for b in range(buckets):
            row = (b + 1) * body
            nets.append((origin[k] * buckets + b, ref[row : row + body, :].astype(f32)))
        row = (buckets + 1) * body
        size = local_micro * dates
        rest = ref[row : row + 2 * size, :].astype(f32)
        spread_ref[pl.ds(origin[k] * local_micro, local_micro)] = (
            rest[:size] + rest[size:]
        ).reshape(local_micro, dates, lanes)
    squares = within
    for i, (at, net) in enumerate(nets):
        coupled = 0.0
        for k, (other_at, other) in enumerate(nets):
            if k != i:
                coupled = coupled + gamma_ref[at, other_at] * other
        squares = squares + net * coupled
    root = jnp.sqrt(squares).reshape(half, dates, lanes)
    lane = lax.broadcasted_iota(jnp.int32, (dates, lanes), 1)
    total = jnp.zeros((dates, lanes), f32)
    for m in range(half):
        live = count_ref[core * half + m]
        margin = jnp.where(lane < live, root[m], f32(0.0))
        margin_ref[m] = margin
        total = total + spread_ref[core * half + m] * margin / live.astype(f32)
    total = jnp.sum(jnp.sum(total, axis=0, keepdims=True), axis=1, keepdims=True)
    out_ref[:local_micro] = margin_ref[pl.ds(place_ref[2], local_micro)]
    out_ref[local_micro] = jnp.broadcast_to(total, (dates, lanes))


def shards(
    transition,
    shocks,
    step_days,
    readout,
    risk_weight,
    correlation,
    cross_gamma,
    discount,
    path_counts,
):
    position = lax.axis_index("date")
    segments = lax.axis_size("date")
    zs = lax.axis_size("bucket")
    z = lax.axis_index("bucket")
    dates, buckets, features, batches, lanes = shocks.shape
    sens = readout.shape[1]
    scales = jnp.sqrt(step_days.astype(f32) / 30.0)
    half = batches // 2
    pieces = half // pair
    width = pair * lanes
    seen_rows = dates * sens
    rows = features + seen_rows
    core = lax.rem(position, 2)
    core_flag = core.astype(jnp.int32).reshape(1)
    stages = (segments // 2).bit_length() - 1
    ups = [lax.rem(position // (2 << s), 2).astype(jnp.int32).reshape(1) for s in range(stages)]
    swap = [(i, i ^ 1) for i in range(segments)]
    smem = pl.BlockSpec(memory_space=pltpu.SMEM)

    vmem = pl.BlockSpec(memory_space=pltpu.VMEM)
    hbm = pl.BlockSpec(memory_space=pltpu.HBM)
    anywhere = pl.BlockSpec(memory_space=pl.ANY)
    small = pltpu.CompilerParams(vmem_limit_bytes=50 * 2**20)
    large = pltpu.CompilerParams(vmem_limit_bytes=50 * 2**20)
    operators = pl.pallas_call(
        functools.partial(operator_kernel, dates),
        out_shape=jax.ShapeDtypeStruct((buckets, rows, features), bf16),
        grid=(buckets,),
        in_specs=[
            pl.BlockSpec((dates, 1, features, features), lambda b: (0, b, 0, 0)),
            pl.BlockSpec((1, sens, features), lambda b: (b, 0, 0)),
        ],
        out_specs=pl.BlockSpec((1, rows, features), lambda b: (b, 0, 0)),
        cost_estimate=cost(2 * buckets * dates * features**3, 2**23),
        compiler_params=pltpu.CompilerParams(vmem_limit_bytes=50 * 2**20),
        name="operators",
    )(transition, readout)

    def local(b, octet, scales):
        return pl.pallas_call(
            functools.partial(local_kernel, dates, b),
            out_shape=jax.ShapeDtypeStruct((pieces, rows, width), bf16),
            in_specs=[smem, smem, hbm, hbm, hbm],
            out_specs=vmem,
            scratch_shapes=[
                pltpu.VMEM((dates, features, half, lanes), bf16),
                pltpu.VMEM((dates, features, features), bf16),
                pltpu.VMEM((sens, features), bf16),
                pltpu.VMEM((features * half, lanes), f32),
                pltpu.VMEM((features, half * lanes), bf16),
                pltpu.SemaphoreType.DMA((dates,)),
                pltpu.SemaphoreType.DMA((dates,)),
                pltpu.SemaphoreType.DMA,
            ],
            compiler_params=large,
            cost_estimate=cost(2 * dates * rows * features * half * lanes // 2, 2**23),
            name="local",
        )(scales, octet, shocks, transition, readout)

    scales = after(scales, operators)
    operators_other = lax.ppermute(operators, "date", swap)
    sent = local(0, 1 - core_flag, scales)
    operators_other = after(operators_other, sent)
    late_half = lax.ppermute(sent, "date", swap)

    block3 = lambda r: pl.BlockSpec((1, r, features), lambda b: (b, 0, 0))
    block, seer, late, part = pl.pallas_call(
        join_operator_kernel,
        out_shape=(
            jax.ShapeDtypeStruct((buckets, features, features), bf16),
            jax.ShapeDtypeStruct((buckets, 2 * seen_rows, features), bf16),
            jax.ShapeDtypeStruct((buckets, rows, features), bf16),
            jax.ShapeDtypeStruct((buckets, features // 2, features), bf16),
        ),
        grid=(buckets,),
        in_specs=[smem, block3(rows), block3(rows)],
        out_specs=(
            block3(features),
            block3(2 * seen_rows),
            block3(rows),
            block3(features // 2),
        ),
        cost_estimate=cost(2 * buckets * rows * features**2, 2**22),
        compiler_params=pltpu.CompilerParams(vmem_limit_bytes=60 * 2**20),
        name="join_operators",
    )(core_flag, operators, operators_other)

    joined_block = block
    combiners = []
    eye = jnp.broadcast_to(jnp.eye(features, dtype=bf16), (buckets, features, features))
    prefix = eye
    prefixes = [eye]
    for s in range(stages - 1):
        far = [(i, i ^ (2 << s)) for i in range(segments)]
        rows_half = features // 2
        if s > 0:
            part = lax.dynamic_slice_in_dim(block, core * rows_half, rows_half, 1)
        if s == 0:
            scales = after(scales, part)
        part = lax.ppermute(part, "date", far)
        if s == 0:
            own = local(0, core_flag, scales)
            part = after(part, own)
        part_other = lax.ppermute(part, "date", swap)
        if s == 0:
            flags = jnp.concatenate([core_flag, ups[0]])
            straight, crossed = part, part_other
            if stages == 2:
                continue
        first = core == 0
        other = jnp.concatenate(
            [jnp.where(first, part, part_other), jnp.where(first, part_other, part)], axis=1
        )
        up = ups[s][0] == 1
        combiners.append(jnp.where(up, block, other))
        if s == 0:
            prefix = jnp.where(up, other, eye)
            prefixes.append(prefix)
        else:
            moved = jnp.einsum("bij,bjk->bik", prefix, other, preferred_element_type=f32)
            prefix = jnp.where(up, moved.astype(bf16), prefix)
            prefixes.append(prefix)
        if s < stages - 2:
            above = jnp.where(up, block, other)
            below = jnp.where(up, other, block)
            block = jnp.einsum(
                "bij,bjk->bik", above, below, preferred_element_type=f32
            ).astype(bf16)

    if stages < 2:
        own = local(0, core_flag, scales)

    ends = []
    seens = []
    table = []
    places = {}
    for b in range(buckets):
        unit = 0
        for size in chunks(pieces, b, buckets):
            for i in range(size * pair):
                places[b, unit * pair + i] = (len(table), i)
            table.append((b, unit, size))
            unit += size
    count = len(table)

    def join_states(b, own, late_half):
        sizes = [size for at, _, size in table if at == b]
        call = pl.pallas_call(
            functools.partial(join_state_kernel, b, sizes),
            out_shape=(jax.ShapeDtypeStruct((pieces, 2 * seen_rows, width), bf16),)
            + tuple(jax.ShapeDtypeStruct((features, size * width), bf16) for size in sizes),
            in_specs=[smem, anywhere, anywhere, anywhere],
            out_specs=(vmem,) * (len(sizes) + 1),
            scratch_shapes=[
                pltpu.VMEM((pieces, rows, width), bf16),
                pltpu.VMEM((pieces, rows, width), bf16),
                pltpu.VMEM((rows, features), bf16),
                pltpu.SemaphoreType.DMA((pieces,)),
                pltpu.SemaphoreType.DMA((pieces,)),
                pltpu.SemaphoreType.DMA,
            ],
            compiler_params=small,
            cost_estimate=cost(2 * rows * features * half * lanes, 2**22),
            name="join_states",
        )
        result = call(core_flag, own, late_half, late)
        seens.append(result[0])
        ends.extend(result[1:])

    weight_column = risk_weight[:, :, None]

    square = pltpu.VMEM((features, features), bf16)

    def first_stage(j, mine, other):
        return pl.pallas_call(
            functools.partial(first_stage_kernel, table[j][0]),
            out_shape=jax.ShapeDtypeStruct(mine.shape, bf16),
            in_specs=[smem, vmem, vmem] + [anywhere] * 3,
            out_specs=vmem,
            scratch_shapes=[square, pltpu.SemaphoreType.DMA((2,))],
            compiler_params=small,
            cost_estimate=cost(2 * features**2 * width, 2**20),
            name="stage",
        )(flags, mine, other, joined_block, straight, crossed)

    def stage(j, up, mine, other, combiner):
        return pl.pallas_call(
            functools.partial(stage_kernel, table[j][0]),
            out_shape=jax.ShapeDtypeStruct(mine.shape, bf16),
            in_specs=[smem, vmem, vmem, vmem],
            out_specs=vmem,
            compiler_params=small,
            cost_estimate=cost(2 * features**2 * width, 2**20),
            name="stage",
        )(up, mine, other, combiner)

    def final(j, up, first, last):
        b, q, size = table[j]
        halves = stages == 2
        prefix = (straight, crossed) if halves else (prefixes[-1],)
        flag = flags if halves else jnp.concatenate([core_flag, jnp.ones((1,), jnp.int32)])
        if not halves:
            first = jnp.where(up[0] == 1, first, jnp.zeros_like(first))
        return pl.pallas_call(
            functools.partial(final_kernel, b, q, 2 * dates, halves),
            out_shape=jax.ShapeDtypeStruct((2, 2 * dates, size * width), f32),
            in_specs=[smem, vmem, vmem] + [anywhere] * (len(prefix) + 2) + [vmem] * 2,
            out_specs=vmem,
            scratch_shapes=[
                square,
                pltpu.VMEM((2 * seen_rows, features), bf16),
                pltpu.VMEM((size, 2 * seen_rows, width), bf16),
                pltpu.SemaphoreType.DMA((4,)),
            ],
            compiler_params=small,
            cost_estimate=cost(4 * features**2 * width, 2**21),
            name="final",
        )(flag, first, last, *prefix, seer, seens[b], weight_column, correlation)

    arrived = [[] for _ in range(stages)]
    leaving = [[] for _ in range(stages)]
    holds = {}
    results = []

    def held(s, j):
        if s == 0:
            return jnp.zeros(arrived[0][j].shape, bf16), jnp.ones((1,), jnp.int32)
        if s == 1:
            return arrived[0][j], ups[0]
        if (s, j) not in holds:
            before, flag = held(s - 1, j)
            before = jnp.where(flag[0] == 1, before, jnp.zeros_like(before)).astype(f32)
            moved = dot(prefixes[s - 1][table[j][0]], arrived[s - 1][j])
            value = jnp.where(ups[s - 1][0] == 1, before + moved, before)
            holds[s, j] = value.astype(bf16)
        return holds[s, j], jnp.ones((1,), jnp.int32)

    def advance(s, behind=None):
        j = len(arrived[s])
        last = s == stages - 1
        bit = 2 << s
        link = [(i, i ^ bit) for i in range(segments) if not (last and i & bit)]
        if s == 0:
            out = ends[j]
        else:
            near = arrived[s - 1][j]
            if behind is not None:
                near = after(near, results[behind])
            if s == 1:
                out = first_stage(j, leaving[0][j], near)
            else:
                out = stage(j, ups[s - 1], leaving[s - 1][j], near, combiners[s - 1])
        if j >= flight:
            out = after(out, arrived[s][j - flight])
        leaving[s].append(out)
        arrived[s].append(lax.ppermute(out, "date", link))

    def finish():
        i = len(results)
        before, flag = held(stages - 1, i)
        results.append(final(i, flag, before, arrived[-1][i]))

    join_states(0, own, late_half)
    for b in range(buckets):
        for at, _, _ in table:
            if at == b:
                advance(0)
        if b + 1 < buckets:
            scales = after(scales, ends[-1])
            sent = local(b + 1, 1 - core_flag, scales)
            late_half = lax.ppermute(sent, "date", swap)
            scales = after(scales, sent)
            for _ in range(early if stages > 1 else 0):
                at = len(arrived[1])
                arrived[0][at] = after(arrived[0][at], sent)
                advance(1)
                scales = after(scales, leaving[1][-1])
            own = local(b + 1, core_flag, scales)
            join_states(b + 1, own, late_half)
    for s in range(1, stages):
        last = s == stages - 1
        if last:
            while len(arrived[s]) < 2:
                advance(s)
            discount, cross_gamma, step_days = lax.optimization_barrier(
                (discount, cross_gamma, step_days, leaving[s][-1])
            )[:3]
            discount = (step_days.astype(f32) / 365.0)[:, None, None] * discount
            discount_other = lax.ppermute(discount, "date", swap)
        while len(arrived[s]) < count:
            j = len(arrived[s])
            while last and len(results) < j - lag:
                finish()
            advance(s, j - lag - 1 if last and j > lag else None)
    while len(results) < count:
        finish()

    local_micro = discount.shape[1]
    both = jnp.where(
        core == 0,
        jnp.stack([discount, discount_other]),
        jnp.stack([discount_other, discount]),
    ).reshape(2 * dates, local_micro, lanes)
    high, low = split(jnp.swapaxes(both, 0, 1))
    carried = jnp.concatenate([high.reshape(-1, lanes), low.reshape(-1, lanes)], axis=0)
    body_rows = (buckets + 1) * half * 2 * dates
    message = pl.pallas_call(
        functools.partial(pack_kernel, places, buckets, half),
        out_shape=jax.ShapeDtypeStruct((body_rows + carried.shape[0], lanes), bf16),
        in_specs=[vmem] * (count + 1),
        out_specs=vmem,
        compiler_params=small,
        name="pack",
    )(*results, carried)
    gathered = [message]
    for k in range(1, zs):
        gathered.append(lax.ppermute(message, "bucket", [(i, (i + k) % zs) for i in range(zs)]))
    gamma = (
        0.5
        * (cross_gamma + cross_gamma.T)
        * (1.0 - jnp.eye(cross_gamma.shape[0], dtype=f32))
    )
    start = z * local_micro
    holder = start // half
    place = jnp.stack([z, core, start - holder * half]).astype(jnp.int32)
    out = pl.pallas_call(
        functools.partial(margin_kernel, buckets, 2 * dates, local_micro, half),
        out_shape=jax.ShapeDtypeStruct((local_micro + 1, 2 * dates, lanes), f32),
        in_specs=[smem] * 3 + [vmem] * zs,
        out_specs=vmem,
        scratch_shapes=[
            pltpu.VMEM((batches, 2 * dates, lanes), f32),
            pltpu.VMEM((half, 2 * dates, lanes), f32),
        ],
        compiler_params=small,
        name="margins",
    )(place, gamma, path_counts, *gathered)
    came = lax.ppermute(out, "date", swap)
    margin = jnp.where(holder == core, out[:local_micro], came[:local_micro])
    margin = lax.dynamic_slice_in_dim(margin, core * dates, dates, 1)
    margin = jnp.swapaxes(margin, 0, 1)
    total = out[local_micro] + came[local_micro]
    step = 2
    while step < segments:
        total = total + lax.ppermute(total, "date", [(i, i ^ step) for i in range(segments)])
        step *= 2
    return (margin, total[0, 0])


def solution(mesh):
    in_specs = (
        P("date", "bucket", None, None),
        P("date", "bucket", None, None, None),
        P("date"),
        P("bucket", None, None),
        P("bucket", None),
        P("bucket", None, None),
        P(),
        P("date", "bucket", None),
        P(),
    )
    out_specs = (P("date", "bucket", None), P())


    return jax.shard_map(shards, mesh=mesh, in_specs=in_specs, out_specs=out_specs, check_vma=False)
```

```python
import functools

import jax
import jax.numpy as jnp
from jax import lax
from jax.experimental import pallas as pl
from jax.experimental.pallas import tpu as pltpu
from jax.sharding import PartitionSpec as P


epsilon = 1e-06
f32 = jnp.float32
bf16 = jnp.bfloat16
pair = 2
flight = 8
lag = 1
early = 1


def chunks(units, bucket, buckets):
    sizes = [2] * (units // 2) + [1] * (units % 2)
    if units % 2 == 0:
        if bucket == 0:
            sizes[:1] = [1, 1]
        elif bucket == buckets - 1:
            sizes[-1:] = [1, 1]
    return sizes


def dot(a, b):
    return jnp.dot(a, b, preferred_element_type=f32)


def split(x):
    high = x.astype(bf16)
    return high, (x - high.astype(f32)).astype(bf16)


def cost(flops, read):
    return pl.CostEstimate(flops=flops, bytes_accessed=read, transcendentals=0)


def after(x, y):
    return lax.optimization_barrier((x, y))[0]


def operator_kernel(dates, a_ref, r_ref, w_ref):
    features = a_ref.shape[-1]
    sens = r_ref.shape[1]
    product = a_ref[0, 0]
    for t in range(dates):
        upper = r_ref[0]
        if t + 1 < dates:
            upper = jnp.concatenate([a_ref[t + 1, 0], upper], axis=0)
        moved = dot(upper, product).astype(bf16)
        row = features + t * sens
        w_ref[0, row : row + sens, :] = moved[-sens:]
        if t + 1 < dates:
            product = moved[:features]
    w_ref[0, :features, :] = product


def local_kernel(
    dates,
    b,
    scale_ref,
    octet_ref,
    x_hbm,
    a_hbm,
    r_hbm,
    out_ref,
    x_ref,
    a_ref,
    r_ref,
    rows_ref,
    state_ref,
    x_sem,
    a_sem,
    r_sem,
):
    features, micro, lanes = x_ref.shape[1:]
    sens = r_hbm.shape[1]
    width = pair * lanes
    pieces = micro // pair
    begin = pl.multiple_of(octet_ref[0] * micro, micro)

    def fetch_x(t):
        return pltpu.make_async_copy(
            x_hbm.at[t, b, :, pl.ds(begin, micro), :], x_ref.at[t], x_sem.at[t]
        )

    def fetch_a(t):
        return pltpu.make_async_copy(a_hbm.at[t, b], a_ref.at[t], a_sem.at[t])

    fetch_r = pltpu.make_async_copy(r_hbm.at[b], r_ref, r_sem)
    for t in range(dates):
        fetch_x(t).start()
        if t:
            fetch_a(t).start()
        else:
            fetch_r.start()
    for t in range(dates):
        fetch_x(t).wait()
        rows_ref[...] = x_ref[t].astype(f32).reshape(features * micro, lanes)
        if t:
            fetch_a(t).wait()
        else:
            fetch_r.wait()
        for q in range(pieces):
            cols = slice(q * width, (q + 1) * width)
            total = scale_ref[t] * jnp.concatenate(
                [rows_ref[pl.ds(q * pair + i, features, stride=micro), :] for i in range(pair)],
                axis=1,
            )
            if t:
                total = total + dot(a_ref[t], state_ref[:, cols])
            state_ref[:, cols] = total.astype(bf16)
        row = features + t * sens
        for q in range(pieces):
            state = state_ref[:, q * width : (q + 1) * width]
            out_ref[q, row : row + sens, :] = dot(r_ref[...], state).astype(bf16)
    for q in range(pieces):
        out_ref[q, :features, :] = state_ref[:, q * width : (q + 1) * width]


def join_operator_kernel(core_ref, mine_ref, other_ref, p_ref, q_ref, late_ref, part_ref):
    features = mine_ref.shape[2]
    first = core_ref[0] == 0
    mine, other = mine_ref[0], other_ref[0]
    early = jnp.where(first, mine, other)
    late = jnp.where(first, other, mine)
    joined = dot(late, early[:features]).astype(bf16)
    p_ref[0] = joined[:features]
    part_ref[0] = jnp.where(first, joined[: features // 2], joined[features // 2 : features])
    seen = late.shape[0] - features
    q_ref[0, :seen, :] = early[features:]
    q_ref[0, seen:, :] = joined[features:]
    late_ref[0] = late


def join_state_kernel(
    b,
    sizes,
    core_ref,
    mine_hbm,
    other_hbm,
    late_hbm,
    seen_ref,
    *refs,
):
    end_refs = refs[:-6]
    mine_ref, other_ref, late_ref, mine_sem, other_sem, late_sem = refs[-6:]
    features = late_ref.shape[1]
    width = mine_ref.shape[2]
    first = core_ref[0] == 0
    fetch = pltpu.make_async_copy(late_hbm.at[b], late_ref, late_sem)
    fetch.start()
    pieces = [
        (
            pltpu.make_async_copy(mine_hbm.at[q], mine_ref.at[q], mine_sem.at[q]),
            pltpu.make_async_copy(other_hbm.at[q], other_ref.at[q], other_sem.at[q]),
        )
        for q in range(sum(sizes))
    ]
    for one, two in pieces:
        one.start()
        two.start()
    fetch.wait()
    late_operator = late_ref[...]
    q = 0
    for end_ref, size in zip(end_refs, sizes):
        for i in range(size):
            for piece in pieces[q]:
                piece.wait()
            mine, other = mine_ref[q], other_ref[q]
            early = jnp.where(first, mine, other)
            late = jnp.where(first, other, mine)
            joined = dot(late_operator, early[:features]) + late.astype(f32)
            seen = late.shape[0] - features
            seen_ref[q, :seen, :] = early[features:]
            seen_ref[q, seen:, :] = joined[features:].astype(bf16)
            end_ref[:, i * width : (i + 1) * width] = joined[:features].astype(bf16)
            q += 1


def far_copies(b, core, part_hbm, part_other_hbm, a_ref, sem):
    half = part_hbm.shape[1]
    near = pl.ds(pl.multiple_of(core * half, half), half)
    away = pl.ds(pl.multiple_of((1 - core) * half, half), half)
    return (
        pltpu.make_async_copy(part_hbm.at[b], a_ref.at[near], sem.at[0]),
        pltpu.make_async_copy(part_other_hbm.at[b], a_ref.at[away], sem.at[1]),
    )


def first_stage_kernel(
    b, flag_ref, mine_ref, other_ref, block_hbm, part_hbm, part_other_hbm, out_ref, a_ref, sem
):
    up = flag_ref[1] == 1

    @pl.when(up)
    def _():
        copy = pltpu.make_async_copy(block_hbm.at[b], a_ref, sem.at[0])
        copy.start()
        copy.wait()

    @pl.when(flag_ref[1] == 0)
    def _():
        copies = far_copies(b, flag_ref[0], part_hbm, part_other_hbm, a_ref, sem)
        for copy in copies:
            copy.start()
        for copy in copies:
            copy.wait()

    mine, other = mine_ref[...], other_ref[...]
    early = jnp.where(up, other, mine)
    late = jnp.where(up, mine, other)
    out_ref[...] = (dot(a_ref[...], early) + late.astype(f32)).astype(bf16)


def stage_kernel(b, up_ref, mine_ref, other_ref, a_ref, out_ref):
    up = up_ref[0] == 1
    mine, other = mine_ref[...], other_ref[...]
    early = jnp.where(up, other, mine)
    late = jnp.where(up, mine, other)
    out_ref[...] = (dot(a_ref[b], early) + late.astype(f32)).astype(bf16)


def final_kernel(b, q, dates, halves, flag_ref, first_ref, last_ref, *refs):
    prefix, (q_hbm, seen_hbm, rw_ref, c_ref, out_ref) = refs[:-9], refs[-9:-4]
    a_ref, q_ref, seen_ref, sem = refs[-4:]
    sens = rw_ref.shape[1]
    width = first_ref.shape[1]
    units = seen_ref.shape[0]
    fetch_q = pltpu.make_async_copy(q_hbm.at[b], q_ref, sem.at[2])
    fetch_seen = pltpu.make_async_copy(seen_hbm.at[pl.ds(q, units)], seen_ref, sem.at[3])
    if halves:
        copies = far_copies(b, flag_ref[0], *prefix, a_ref, sem)
    else:
        copies = (pltpu.make_async_copy(prefix[0].at[b], a_ref, sem.at[0]),)
    for copy in copies:
        copy.start()
    fetch_q.start()
    fetch_seen.start()
    for copy in copies:
        copy.wait()
    up = flag_ref[1] == 1
    last = last_ref[...]
    moved = first_ref[...].astype(f32) + dot(a_ref[...], last)
    entering = jnp.where(up, moved.astype(bf16), last)
    fetch_q.wait()
    seen = dot(q_ref[...], entering)
    fetch_seen.wait()
    seen = seen + jnp.concatenate([seen_ref[i] for i in range(units)], axis=1).astype(f32)
    weight = rw_ref[b]
    ws = jnp.concatenate(
        [weight * seen[t * sens : (t + 1) * sens] for t in range(dates)], axis=1
    )
    c_high, c_low = split(c_ref[b])
    w_high, w_low = split(ws)
    mixed = dot(
        jnp.concatenate([c_high, c_low, c_high], axis=1),
        jnp.concatenate([w_high, w_high, w_low], axis=0),
    )
    within = jnp.sum(ws * mixed, axis=0, keepdims=True) + epsilon
    root = jnp.sqrt(within)
    net = jnp.clip(jnp.sum(ws, axis=0, keepdims=True), -root, root)
    for t in range(dates):
        out_ref[0, t : t + 1, :] = within[:, t * width : (t + 1) * width]
        out_ref[1, t : t + 1, :] = net[:, t * width : (t + 1) * width]


def pack_kernel(places, buckets, half, *refs):
    stats, discount_ref, out_ref = refs[:-2], refs[-2], refs[-1]
    dates = stats[0].shape[1]
    lanes = out_ref.shape[1]

    def value(kind, b, m):
        j, lane = places[b, m]
        return stats[j][kind, :, lane * lanes : (lane + 1) * lanes]

    for m in range(0, half, 2):
        block = [[value(1, b, m + i) for i in range(2)] for b in range(buckets)]
        block.insert(0, [sum(value(0, b, m + i) for b in range(buckets)) for i in range(2)])
        for r, parts in enumerate(block):
            row = (r * half + m) * dates
            out_ref[row : row + 2 * dates, :] = jnp.concatenate(parts, axis=0).astype(bf16)
    out_ref[(buckets + 1) * half * dates :, :] = discount_ref[...]


def margin_kernel(
    buckets, dates, local_micro, half, place_ref, gamma_ref, count_ref, *refs
):
    messages, (out_ref, spread_ref, margin_ref) = refs[:-3], refs[-3:]
    zs = len(messages)
    lanes = out_ref.shape[2]
    body = half * dates
    shard, core = place_ref[0], place_ref[1]
    origin = [lax.rem(shard - k + zs, zs) for k in range(zs)]
    within = 0.0
    nets = []
    for k, ref in enumerate(messages):
        within = within + ref[:body, :].astype(f32)
        for b in range(buckets):
            row = (b + 1) * body
            nets.append((origin[k] * buckets + b, ref[row : row + body, :].astype(f32)))
        row = (buckets + 1) * body
        size = local_micro * dates
        rest = ref[row : row + 2 * size, :].astype(f32)
        spread_ref[pl.ds(origin[k] * local_micro, local_micro)] = (
            rest[:size] + rest[size:]
        ).reshape(local_micro, dates, lanes)
    squares = within
    for i, (at, net) in enumerate(nets):
        coupled = 0.0
        for k, (other_at, other) in enumerate(nets):
            if k != i:
                coupled = coupled + gamma_ref[at, other_at] * other
        squares = squares + net * coupled
    root = jnp.sqrt(squares).reshape(half, dates, lanes)
    lane = lax.broadcasted_iota(jnp.int32, (dates, lanes), 1)
    total = jnp.zeros((dates, lanes), f32)
    for m in range(half):
        live = count_ref[core * half + m]
        margin = jnp.where(lane < live, root[m], f32(0.0))
        margin_ref[m] = margin
        total = total + spread_ref[core * half + m] * margin / live.astype(f32)
    total = jnp.sum(jnp.sum(total, axis=0, keepdims=True), axis=1, keepdims=True)
    out_ref[:local_micro] = margin_ref[pl.ds(place_ref[2], local_micro)]
    out_ref[local_micro] = jnp.broadcast_to(total, (dates, lanes))


def shards(
    transition,
    shocks,
    step_days,
    readout,
    risk_weight,
    correlation,
    cross_gamma,
    discount,
    path_counts,
):
    position = lax.axis_index("date")
    segments = lax.axis_size("date")
    zs = lax.axis_size("bucket")
    z = lax.axis_index("bucket")
    dates, buckets, features, batches, lanes = shocks.shape
    sens = readout.shape[1]
    scales = jnp.sqrt(step_days.astype(f32) / 30.0)
    half = batches // 2
    pieces = half // pair
    width = pair * lanes
    seen_rows = dates * sens
    rows = features + seen_rows
    core = lax.rem(position, 2)
    core_flag = core.astype(jnp.int32).reshape(1)
    stages = (segments // 2).bit_length() - 1
    ups = [lax.rem(position // (2 << s), 2).astype(jnp.int32).reshape(1) for s in range(stages)]
    swap = [(i, i ^ 1) for i in range(segments)]
    smem = pl.BlockSpec(memory_space=pltpu.SMEM)

    vmem = pl.BlockSpec(memory_space=pltpu.VMEM)
    hbm = pl.BlockSpec(memory_space=pltpu.HBM)
    anywhere = pl.BlockSpec(memory_space=pl.ANY)
    small = pltpu.CompilerParams(vmem_limit_bytes=50 * 2**20)
    large = pltpu.CompilerParams(vmem_limit_bytes=50 * 2**20)
    operators = pl.pallas_call(
        functools.partial(operator_kernel, dates),
        out_shape=jax.ShapeDtypeStruct((buckets, rows, features), bf16),
        grid=(buckets,),
        in_specs=[
            pl.BlockSpec((dates, 1, features, features), lambda b: (0, b, 0, 0)),
            pl.BlockSpec((1, sens, features), lambda b: (b, 0, 0)),
        ],
        out_specs=pl.BlockSpec((1, rows, features), lambda b: (b, 0, 0)),
        cost_estimate=cost(2 * buckets * dates * features**3, 2**23),
        compiler_params=pltpu.CompilerParams(vmem_limit_bytes=50 * 2**20),
        name="operators",
    )(transition, readout)

    def local(b, octet, scales):
        return pl.pallas_call(
            functools.partial(local_kernel, dates, b),
            out_shape=jax.ShapeDtypeStruct((pieces, rows, width), bf16),
            in_specs=[smem, smem, hbm, hbm, hbm],
            out_specs=vmem,
            scratch_shapes=[
                pltpu.VMEM((dates, features, half, lanes), bf16),
                pltpu.VMEM((dates, features, features), bf16),
                pltpu.VMEM((sens, features), bf16),
                pltpu.VMEM((features * half, lanes), f32),
                pltpu.VMEM((features, half * lanes), bf16),
                pltpu.SemaphoreType.DMA((dates,)),
                pltpu.SemaphoreType.DMA((dates,)),
                pltpu.SemaphoreType.DMA,
            ],
            compiler_params=large,
            cost_estimate=cost(2 * dates * rows * features * half * lanes // 2, 2**23),
            name="local",
        )(scales, octet, shocks, transition, readout)

    scales = after(scales, operators)
    operators_other = lax.ppermute(operators, "date", swap)
    sent = local(0, 1 - core_flag, scales)
    operators_other = after(operators_other, sent)
    late_half = lax.ppermute(sent, "date", swap)

    block3 = lambda r: pl.BlockSpec((1, r, features), lambda b: (b, 0, 0))
    block, seer, late, part = pl.pallas_call(
        join_operator_kernel,
        out_shape=(
            jax.ShapeDtypeStruct((buckets, features, features), bf16),
            jax.ShapeDtypeStruct((buckets, 2 * seen_rows, features), bf16),
            jax.ShapeDtypeStruct((buckets, rows, features), bf16),
            jax.ShapeDtypeStruct((buckets, features // 2, features), bf16),
        ),
        grid=(buckets,),
        in_specs=[smem, block3(rows), block3(rows)],
        out_specs=(
            block3(features),
            block3(2 * seen_rows),
            block3(rows),
            block3(features // 2),
        ),
        cost_estimate=cost(2 * buckets * rows * features**2, 2**22),
        compiler_params=pltpu.CompilerParams(vmem_limit_bytes=60 * 2**20),
        name="join_operators",
    )(core_flag, operators, operators_other)

    joined_block = block
    combiners = []
    eye = jnp.broadcast_to(jnp.eye(features, dtype=bf16), (buckets, features, features))
    prefix = eye
    prefixes = [eye]
    for s in range(stages - 1):
        far = [(i, i ^ (2 << s)) for i in range(segments)]
        rows_half = features // 2
        if s > 0:
            part = lax.dynamic_slice_in_dim(block, core * rows_half, rows_half, 1)
        if s == 0:
            scales = after(scales, part)
        part = lax.ppermute(part, "date", far)
        if s == 0:
            own = local(0, core_flag, scales)
            part = after(part, own)
        part_other = lax.ppermute(part, "date", swap)
        if s == 0:
            flags = jnp.concatenate([core_flag, ups[0]])
            straight, crossed = part, part_other
            if stages == 2:
                continue
        first = core == 0
        other = jnp.concatenate(
            [jnp.where(first, part, part_other), jnp.where(first, part_other, part)], axis=1
        )
        up = ups[s][0] == 1
        combiners.append(jnp.where(up, block, other))
        if s == 0:
            prefix = jnp.where(up, other, eye)
            prefixes.append(prefix)
        else:
            moved = jnp.einsum("bij,bjk->bik", prefix, other, preferred_element_type=f32)
            prefix = jnp.where(up, moved.astype(bf16), prefix)
            prefixes.append(prefix)
        if s < stages - 2:
            above = jnp.where(up, block, other)
            below = jnp.where(up, other, block)
            block = jnp.einsum(
                "bij,bjk->bik", above, below, preferred_element_type=f32
            ).astype(bf16)

    if stages < 2:
        own = local(0, core_flag, scales)

    ends = []
    seens = []
    table = []
    places = {}
    for b in range(buckets):
        unit = 0
        for size in chunks(pieces, b, buckets):
            for i in range(size * pair):
                places[b, unit * pair + i] = (len(table), i)
            table.append((b, unit, size))
            unit += size
    count = len(table)

    def join_states(b, own, late_half):
        sizes = [size for at, _, size in table if at == b]
        call = pl.pallas_call(
            functools.partial(join_state_kernel, b, sizes),
            out_shape=(jax.ShapeDtypeStruct((pieces, 2 * seen_rows, width), bf16),)
            + tuple(jax.ShapeDtypeStruct((features, size * width), bf16) for size in sizes),
            in_specs=[smem, anywhere, anywhere, anywhere],
            out_specs=(vmem,) * (len(sizes) + 1),
            scratch_shapes=[
                pltpu.VMEM((pieces, rows, width), bf16),
                pltpu.VMEM((pieces, rows, width), bf16),
                pltpu.VMEM((rows, features), bf16),
                pltpu.SemaphoreType.DMA((pieces,)),
                pltpu.SemaphoreType.DMA((pieces,)),
                pltpu.SemaphoreType.DMA,
            ],
            compiler_params=small,
            cost_estimate=cost(2 * rows * features * half * lanes, 2**22),
            name="join_states",
        )
        result = call(core_flag, own, late_half, late)
        seens.append(result[0])
        ends.extend(result[1:])

    weight_column = risk_weight[:, :, None]

    square = pltpu.VMEM((features, features), bf16)

    def first_stage(j, mine, other):
        return pl.pallas_call(
            functools.partial(first_stage_kernel, table[j][0]),
            out_shape=jax.ShapeDtypeStruct(mine.shape, bf16),
            in_specs=[smem, vmem, vmem] + [anywhere] * 3,
            out_specs=vmem,
            scratch_shapes=[square, pltpu.SemaphoreType.DMA((2,))],
            compiler_params=small,
            cost_estimate=cost(2 * features**2 * width, 2**20),
            name="stage",
        )(flags, mine, other, joined_block, straight, crossed)

    def stage(j, up, mine, other, combiner):
        return pl.pallas_call(
            functools.partial(stage_kernel, table[j][0]),
            out_shape=jax.ShapeDtypeStruct(mine.shape, bf16),
            in_specs=[smem, vmem, vmem, vmem],
            out_specs=vmem,
            compiler_params=small,
            cost_estimate=cost(2 * features**2 * width, 2**20),
            name="stage",
        )(up, mine, other, combiner)

    def final(j, up, first, last):
        b, q, size = table[j]
        halves = stages == 2
        prefix = (straight, crossed) if halves else (prefixes[-1],)
        flag = flags if halves else jnp.concatenate([core_flag, jnp.ones((1,), jnp.int32)])
        if not halves:
            first = jnp.where(up[0] == 1, first, jnp.zeros_like(first))
        return pl.pallas_call(
            functools.partial(final_kernel, b, q, 2 * dates, halves),
            out_shape=jax.ShapeDtypeStruct((2, 2 * dates, size * width), f32),
            in_specs=[smem, vmem, vmem] + [anywhere] * (len(prefix) + 2) + [vmem] * 2,
            out_specs=vmem,
            scratch_shapes=[
                square,
                pltpu.VMEM((2 * seen_rows, features), bf16),
                pltpu.VMEM((size, 2 * seen_rows, width), bf16),
                pltpu.SemaphoreType.DMA((4,)),
            ],
            compiler_params=small,
            cost_estimate=cost(4 * features**2 * width, 2**21),
            name="final",
        )(flag, first, last, *prefix, seer, seens[b], weight_column, correlation)

    arrived = [[] for _ in range(stages)]
    leaving = [[] for _ in range(stages)]
    holds = {}
    results = []

    def held(s, j):
        if s == 0:
            return jnp.zeros(arrived[0][j].shape, bf16), jnp.ones((1,), jnp.int32)
        if s == 1:
            return arrived[0][j], ups[0]
        if (s, j) not in holds:
            before, flag = held(s - 1, j)
            before = jnp.where(flag[0] == 1, before, jnp.zeros_like(before)).astype(f32)
            moved = dot(prefixes[s - 1][table[j][0]], arrived[s - 1][j])
            value = jnp.where(ups[s - 1][0] == 1, before + moved, before)
            holds[s, j] = value.astype(bf16)
        return holds[s, j], jnp.ones((1,), jnp.int32)

    def advance(s, behind=None):
        j = len(arrived[s])
        last = s == stages - 1
        bit = 2 << s
        link = [(i, i ^ bit) for i in range(segments) if not (last and i & bit)]
        if s == 0:
            out = ends[j]
        else:
            near = arrived[s - 1][j]
            if behind is not None:
                near = after(near, results[behind])
            if s == 1:
                out = first_stage(j, leaving[0][j], near)
            else:
                out = stage(j, ups[s - 1], leaving[s - 1][j], near, combiners[s - 1])
        if j >= flight:
            out = after(out, arrived[s][j - flight])
        leaving[s].append(out)
        arrived[s].append(lax.ppermute(out, "date", link))

    def finish():
        i = len(results)
        if results:
            arrived[-1][i] = after(arrived[-1][i], results[-1])
        before, flag = held(stages - 1, i)
        results.append(final(i, flag, before, arrived[-1][i]))

    join_states(0, own, late_half)
    for b in range(buckets):
        for at, _, _ in table:
            if at == b:
                advance(0)
        if b + 1 < buckets:
            scales = after(scales, ends[-1])
            sent = local(b + 1, 1 - core_flag, scales)
            late_half = lax.ppermute(sent, "date", swap)
            scales = after(scales, sent)
            for _ in range(early if stages > 1 else 0):
                at = len(arrived[1])
                arrived[0][at] = after(arrived[0][at], sent)
                advance(1)
                scales = after(scales, leaving[1][-1])
            own = local(b + 1, core_flag, scales)
            join_states(b + 1, own, late_half)
    for s in range(1, stages):
        last = s == stages - 1
        if last:
            while len(arrived[s]) < 2:
                advance(s)
            discount, cross_gamma, step_days = lax.optimization_barrier(
                (discount, cross_gamma, step_days, leaving[s][-1])
            )[:3]
            discount = (step_days.astype(f32) / 365.0)[:, None, None] * discount
            discount_other = lax.ppermute(discount, "date", swap)
        while len(arrived[s]) < count:
            j = len(arrived[s])
            while last and len(results) < j - lag:
                finish()
            advance(s)
    while len(results) < count:
        finish()

    local_micro = discount.shape[1]
    both = jnp.where(
        core == 0,
        jnp.stack([discount, discount_other]),
        jnp.stack([discount_other, discount]),
    ).reshape(2 * dates, local_micro, lanes)
    high, low = split(jnp.swapaxes(both, 0, 1))
    carried = jnp.concatenate([high.reshape(-1, lanes), low.reshape(-1, lanes)], axis=0)
    body_rows = (buckets + 1) * half * 2 * dates
    message = pl.pallas_call(
        functools.partial(pack_kernel, places, buckets, half),
        out_shape=jax.ShapeDtypeStruct((body_rows + carried.shape[0], lanes), bf16),
        in_specs=[vmem] * (count + 1),
        out_specs=vmem,
        compiler_params=small,
        name="pack",
    )(*results, carried)
    gathered = [message]
    for k in range(1, zs):
        gathered.append(lax.ppermute(message, "bucket", [(i, (i + k) % zs) for i in range(zs)]))
    gamma = (
        0.5
        * (cross_gamma + cross_gamma.T)
        * (1.0 - jnp.eye(cross_gamma.shape[0], dtype=f32))
    )
    start = z * local_micro
    holder = start // half
    place = jnp.stack([z, core, start - holder * half]).astype(jnp.int32)
    out = pl.pallas_call(
        functools.partial(margin_kernel, buckets, 2 * dates, local_micro, half),
        out_shape=jax.ShapeDtypeStruct((local_micro + 1, 2 * dates, lanes), f32),
        in_specs=[smem] * 3 + [vmem] * zs,
        out_specs=vmem,
        scratch_shapes=[
            pltpu.VMEM((batches, 2 * dates, lanes), f32),
            pltpu.VMEM((half, 2 * dates, lanes), f32),
        ],
        compiler_params=small,
        name="margins",
    )(place, gamma, path_counts, *gathered)
    came = lax.ppermute(out, "date", swap)
    margin = jnp.where(holder == core, out[:local_micro], came[:local_micro])
    margin = lax.dynamic_slice_in_dim(margin, core * dates, dates, 1)
    margin = jnp.swapaxes(margin, 0, 1)
    total = out[local_micro] + came[local_micro]
    step = 2
    while step < segments:
        total = total + lax.ppermute(total, "date", [(i, i ^ step) for i in range(segments)])
        step *= 2
    return (margin, total[0, 0])


def solution(mesh):
    in_specs = (
        P("date", "bucket", None, None),
        P("date", "bucket", None, None, None),
        P("date"),
        P("bucket", None, None),
        P("bucket", None),
        P("bucket", None, None),
        P(),
        P("date", "bucket", None),
        P(),
    )
    out_specs = (P("date", "bucket", None), P())


    return jax.shard_map(shards, mesh=mesh, in_specs=in_specs, out_specs=out_specs, check_vma=False)
```

```python
import functools

import jax
import jax.numpy as jnp
from jax import lax
from jax.experimental import pallas as pl
from jax.experimental.pallas import tpu as pltpu
from jax.sharding import PartitionSpec as P


epsilon = 1e-06
f32 = jnp.float32
bf16 = jnp.bfloat16
pair = 2
flight = 8
lag = 1
early = 1


def chunks(units, bucket, buckets):
    sizes = [2] * (units // 2) + [1] * (units % 2)
    if units % 2 == 0:
        if bucket == 0:
            sizes[:1] = [1, 1]
        elif bucket == buckets - 1:
            sizes[-1:] = [1, 1]
    return sizes


def dot(a, b):
    return jnp.dot(a, b, preferred_element_type=f32)


def split(x):
    high = x.astype(bf16)
    return high, (x - high.astype(f32)).astype(bf16)


def cost(flops, read):
    return pl.CostEstimate(flops=flops, bytes_accessed=read, transcendentals=0)


def after(x, y):
    return lax.optimization_barrier((x, y))[0]


def operator_kernel(dates, a_ref, r_ref, w_ref):
    features = a_ref.shape[-1]
    sens = r_ref.shape[1]
    product = a_ref[0, 0]
    for t in range(dates):
        upper = r_ref[0]
        if t + 1 < dates:
            upper = jnp.concatenate([a_ref[t + 1, 0], upper], axis=0)
        moved = dot(upper, product).astype(bf16)
        row = features + t * sens
        w_ref[0, row : row + sens, :] = moved[-sens:]
        if t + 1 < dates:
            product = moved[:features]
    w_ref[0, :features, :] = product


def local_kernel(
    dates,
    b,
    scale_ref,
    octet_ref,
    x_hbm,
    a_hbm,
    r_hbm,
    out_ref,
    x_ref,
    a_ref,
    r_ref,
    rows_ref,
    state_ref,
    x_sem,
    a_sem,
    r_sem,
):
    features, micro, lanes = x_ref.shape[1:]
    sens = r_hbm.shape[1]
    width = pair * lanes
    pieces = micro // pair
    begin = pl.multiple_of(octet_ref[0] * micro, micro)

    def fetch_x(t):
        return pltpu.make_async_copy(
            x_hbm.at[t, b, :, pl.ds(begin, micro), :], x_ref.at[t], x_sem.at[t]
        )

    def fetch_a(t):
        return pltpu.make_async_copy(a_hbm.at[t, b], a_ref.at[t], a_sem.at[t])

    fetch_r = pltpu.make_async_copy(r_hbm.at[b], r_ref, r_sem)
    for t in range(dates):
        fetch_x(t).start()
        if t:
            fetch_a(t).start()
        else:
            fetch_r.start()
    for t in range(dates):
        fetch_x(t).wait()
        rows_ref[...] = x_ref[t].astype(f32).reshape(features * micro, lanes)
        if t:
            fetch_a(t).wait()
        else:
            fetch_r.wait()
        for q in range(pieces):
            cols = slice(q * width, (q + 1) * width)
            total = scale_ref[t] * jnp.concatenate(
                [rows_ref[pl.ds(q * pair + i, features, stride=micro), :] for i in range(pair)],
                axis=1,
            )
            if t:
                total = total + dot(a_ref[t], state_ref[:, cols])
            state_ref[:, cols] = total.astype(bf16)
        row = features + t * sens
        for q in range(pieces):
            state = state_ref[:, q * width : (q + 1) * width]
            out_ref[q, row : row + sens, :] = dot(r_ref[...], state).astype(bf16)
    for q in range(pieces):
        out_ref[q, :features, :] = state_ref[:, q * width : (q + 1) * width]


def join_operator_kernel(core_ref, mine_ref, other_ref, p_ref, q_ref, part_ref):
    features = mine_ref.shape[2]
    first = core_ref[0] == 0
    mine, other = mine_ref[0], other_ref[0]
    early = jnp.where(first, mine, other)
    late = jnp.where(first, other, mine)
    joined = dot(late, early[:features]).astype(bf16)
    p_ref[0] = joined[:features]
    part_ref[0] = jnp.where(first, joined[: features // 2], joined[features // 2 : features])
    seen = late.shape[0] - features
    q_ref[0, :seen, :] = early[features:]
    q_ref[0, seen:, :] = joined[features:]


def join_state_kernel(
    b,
    begin,
    sizes,
    core_ref,
    mine_hbm,
    other_hbm,
    operator_hbm,
    operator_other_hbm,
    seen_ref,
    *refs,
):
    end_refs = refs[:-6]
    mine_ref, other_ref, late_ref, mine_sem, other_sem, late_sem = refs[-6:]
    features = late_ref.shape[1]
    width = mine_ref.shape[2]
    first = core_ref[0] == 0

    @pl.when(first)
    def _():
        pltpu.make_async_copy(operator_other_hbm.at[b], late_ref, late_sem).start()

    @pl.when(core_ref[0] != 0)
    def _():
        pltpu.make_async_copy(operator_hbm.at[b], late_ref, late_sem).start()

    pieces = [
        (
            pltpu.make_async_copy(mine_hbm.at[begin + q], mine_ref.at[q], mine_sem.at[q]),
            pltpu.make_async_copy(other_hbm.at[begin + q], other_ref.at[q], other_sem.at[q]),
        )
        for q in range(sum(sizes))
    ]
    for one, two in pieces:
        one.start()
        two.start()
    pltpu.make_async_copy(operator_hbm.at[b], late_ref, late_sem).wait()
    late_operator = late_ref[...]
    q = 0
    for end_ref, size in zip(end_refs, sizes):
        for i in range(size):
            for piece in pieces[q]:
                piece.wait()
            mine, other = mine_ref[q], other_ref[q]
            early = jnp.where(first, mine, other)
            late = jnp.where(first, other, mine)
            joined = dot(late_operator, early[:features]) + late.astype(f32)
            seen = late.shape[0] - features
            seen_ref[q, :seen, :] = early[features:]
            seen_ref[q, seen:, :] = joined[features:].astype(bf16)
            end_ref[:, i * width : (i + 1) * width] = joined[:features].astype(bf16)
            q += 1


def far_copies(b, core, part_hbm, part_other_hbm, a_ref, sem):
    half = part_hbm.shape[1]
    near = pl.ds(pl.multiple_of(core * half, half), half)
    away = pl.ds(pl.multiple_of((1 - core) * half, half), half)
    return (
        pltpu.make_async_copy(part_hbm.at[b], a_ref.at[near], sem.at[0]),
        pltpu.make_async_copy(part_other_hbm.at[b], a_ref.at[away], sem.at[1]),
    )


def first_stage_kernel(
    b, flag_ref, mine_ref, other_ref, block_hbm, part_hbm, part_other_hbm, out_ref, a_ref, sem
):
    up = flag_ref[1] == 1

    @pl.when(up)
    def _():
        copy = pltpu.make_async_copy(block_hbm.at[b], a_ref, sem.at[0])
        copy.start()
        copy.wait()

    @pl.when(flag_ref[1] == 0)
    def _():
        copies = far_copies(b, flag_ref[0], part_hbm, part_other_hbm, a_ref, sem)
        for copy in copies:
            copy.start()
        for copy in copies:
            copy.wait()

    mine, other = mine_ref[...], other_ref[...]
    early = jnp.where(up, other, mine)
    late = jnp.where(up, mine, other)
    out_ref[...] = (dot(a_ref[...], early) + late.astype(f32)).astype(bf16)


def stage_kernel(b, up_ref, mine_ref, other_ref, a_ref, out_ref):
    up = up_ref[0] == 1
    mine, other = mine_ref[...], other_ref[...]
    early = jnp.where(up, other, mine)
    late = jnp.where(up, mine, other)
    out_ref[...] = (dot(a_ref[b], early) + late.astype(f32)).astype(bf16)


def final_kernel(b, q, dates, halves, flag_ref, first_ref, last_ref, *refs):
    prefix, (q_hbm, seen_hbm, rw_ref, c_ref, out_ref) = refs[:-9], refs[-9:-4]
    a_ref, q_ref, seen_ref, sem = refs[-4:]
    sens = rw_ref.shape[1]
    width = first_ref.shape[1]
    units = seen_ref.shape[0]
    fetch_q = pltpu.make_async_copy(q_hbm.at[b], q_ref, sem.at[2])
    fetch_seen = pltpu.make_async_copy(seen_hbm.at[pl.ds(q, units)], seen_ref, sem.at[3])
    if halves:
        copies = far_copies(b, flag_ref[0], *prefix, a_ref, sem)
    else:
        copies = (pltpu.make_async_copy(prefix[0].at[b], a_ref, sem.at[0]),)
    for copy in copies:
        copy.start()
    fetch_q.start()
    fetch_seen.start()
    for copy in copies:
        copy.wait()
    up = flag_ref[1] == 1
    last = last_ref[...]
    moved = first_ref[...].astype(f32) + dot(a_ref[...], last)
    entering = jnp.where(up, moved.astype(bf16), last)
    fetch_q.wait()
    seen = dot(q_ref[...], entering)
    fetch_seen.wait()
    seen = seen + jnp.concatenate([seen_ref[i] for i in range(units)], axis=1).astype(f32)
    weight = rw_ref[b]
    ws = jnp.concatenate(
        [weight * seen[t * sens : (t + 1) * sens] for t in range(dates)], axis=1
    )
    c_high, c_low = split(c_ref[b])
    w_high, w_low = split(ws)
    mixed = dot(
        jnp.concatenate([c_high, c_low, c_high], axis=1),
        jnp.concatenate([w_high, w_high, w_low], axis=0),
    )
    within = jnp.sum(ws * mixed, axis=0, keepdims=True) + epsilon
    root = jnp.sqrt(within)
    net = jnp.clip(jnp.sum(ws, axis=0, keepdims=True), -root, root)
    for t in range(dates):
        out_ref[0, t : t + 1, :] = within[:, t * width : (t + 1) * width]
        out_ref[1, t : t + 1, :] = net[:, t * width : (t + 1) * width]


def pack_kernel(places, buckets, half, *refs):
    stats, discount_ref, out_ref = refs[:-2], refs[-2], refs[-1]
    dates = stats[0].shape[1]
    lanes = out_ref.shape[1]

    def value(kind, b, m):
        j, lane = places[b, m]
        return stats[j][kind, :, lane * lanes : (lane + 1) * lanes]

    for m in range(0, half, 2):
        block = [[value(1, b, m + i) for i in range(2)] for b in range(buckets)]
        block.insert(0, [sum(value(0, b, m + i) for b in range(buckets)) for i in range(2)])
        for r, parts in enumerate(block):
            row = (r * half + m) * dates
            out_ref[row : row + 2 * dates, :] = jnp.concatenate(parts, axis=0).astype(bf16)
    out_ref[(buckets + 1) * half * dates :, :] = discount_ref[...]


def margin_kernel(
    buckets, dates, local_micro, half, place_ref, gamma_ref, count_ref, *refs
):
    messages, (out_ref, spread_ref, margin_ref) = refs[:-3], refs[-3:]
    zs = len(messages)
    lanes = out_ref.shape[2]
    body = half * dates
    shard, core = place_ref[0], place_ref[1]
    origin = [lax.rem(shard - k + zs, zs) for k in range(zs)]
    within = 0.0
    nets = []
    for k, ref in enumerate(messages):
        within = within + ref[:body, :].astype(f32)
        for b in range(buckets):
            row = (b + 1) * body
            nets.append((origin[k] * buckets + b, ref[row : row + body, :].astype(f32)))
        row = (buckets + 1) * body
        size = local_micro * dates
        rest = ref[row : row + 2 * size, :].astype(f32)
        spread_ref[pl.ds(origin[k] * local_micro, local_micro)] = (
            rest[:size] + rest[size:]
        ).reshape(local_micro, dates, lanes)
    squares = within
    for i, (at, net) in enumerate(nets):
        coupled = 0.0
        for k, (other_at, other) in enumerate(nets):
            if k != i:
                coupled = coupled + gamma_ref[at, other_at] * other
        squares = squares + net * coupled
    root = jnp.sqrt(squares).reshape(half, dates, lanes)
    lane = lax.broadcasted_iota(jnp.int32, (dates, lanes), 1)
    total = jnp.zeros((dates, lanes), f32)
    for m in range(half):
        live = count_ref[core * half + m]
        margin = jnp.where(lane < live, root[m], f32(0.0))
        margin_ref[m] = margin
        total = total + spread_ref[core * half + m] * margin / live.astype(f32)
    total = jnp.sum(jnp.sum(total, axis=0, keepdims=True), axis=1, keepdims=True)
    out_ref[:local_micro] = margin_ref[pl.ds(place_ref[2], local_micro)]
    out_ref[local_micro] = jnp.broadcast_to(total, (dates, lanes))


def shards(
    transition,
    shocks,
    step_days,
    readout,
    risk_weight,
    correlation,
    cross_gamma,
    discount,
    path_counts,
):
    position = lax.axis_index("date")
    segments = lax.axis_size("date")
    zs = lax.axis_size("bucket")
    z = lax.axis_index("bucket")
    dates, buckets, features, batches, lanes = shocks.shape
    sens = readout.shape[1]
    scales = jnp.sqrt(step_days.astype(f32) / 30.0)
    half = batches // 2
    pieces = half // pair
    width = pair * lanes
    seen_rows = dates * sens
    rows = features + seen_rows
    core = lax.rem(position, 2)
    core_flag = core.astype(jnp.int32).reshape(1)
    stages = (segments // 2).bit_length() - 1
    ups = [lax.rem(position // (2 << s), 2).astype(jnp.int32).reshape(1) for s in range(stages)]
    swap = [(i, i ^ 1) for i in range(segments)]
    smem = pl.BlockSpec(memory_space=pltpu.SMEM)

    vmem = pl.BlockSpec(memory_space=pltpu.VMEM)
    hbm = pl.BlockSpec(memory_space=pltpu.HBM)
    anywhere = pl.BlockSpec(memory_space=pl.ANY)
    small = pltpu.CompilerParams(vmem_limit_bytes=50 * 2**20)
    large = pltpu.CompilerParams(vmem_limit_bytes=50 * 2**20)
    operators = pl.pallas_call(
        functools.partial(operator_kernel, dates),
        out_shape=jax.ShapeDtypeStruct((buckets, rows, features), bf16),
        grid=(buckets,),
        in_specs=[
            pl.BlockSpec((dates, 1, features, features), lambda b: (0, b, 0, 0)),
            pl.BlockSpec((1, sens, features), lambda b: (b, 0, 0)),
        ],
        out_specs=pl.BlockSpec((1, rows, features), lambda b: (b, 0, 0)),
        cost_estimate=cost(2 * buckets * dates * features**3, 2**23),
        compiler_params=pltpu.CompilerParams(vmem_limit_bytes=50 * 2**20),
        name="operators",
    )(transition, readout)

    def local(b, octet, scales):
        return pl.pallas_call(
            functools.partial(local_kernel, dates, b),
            out_shape=jax.ShapeDtypeStruct((pieces, rows, width), bf16),
            in_specs=[smem, smem, hbm, hbm, hbm],
            out_specs=vmem,
            scratch_shapes=[
                pltpu.VMEM((dates, features, half, lanes), bf16),
                pltpu.VMEM((dates, features, features), bf16),
                pltpu.VMEM((sens, features), bf16),
                pltpu.VMEM((features * half, lanes), f32),
                pltpu.VMEM((features, half * lanes), bf16),
                pltpu.SemaphoreType.DMA((dates,)),
                pltpu.SemaphoreType.DMA((dates,)),
                pltpu.SemaphoreType.DMA,
            ],
            compiler_params=large,
            cost_estimate=cost(2 * dates * rows * features * half * lanes // 2, 2**23),
            name="local",
        )(scales, octet, shocks, transition, readout)

    scales = after(scales, operators)
    operators_other = lax.ppermute(operators, "date", swap)
    sent = local(0, 1 - core_flag, scales)
    operators_other = after(operators_other, sent)
    late_half = lax.ppermute(sent, "date", swap)

    block3 = lambda r: pl.BlockSpec((1, r, features), lambda b: (b, 0, 0))
    block, seer, part = pl.pallas_call(
        join_operator_kernel,
        out_shape=(
            jax.ShapeDtypeStruct((buckets, features, features), bf16),
            jax.ShapeDtypeStruct((buckets, 2 * seen_rows, features), bf16),
            jax.ShapeDtypeStruct((buckets, features // 2, features), bf16),
        ),
        grid=(buckets,),
        in_specs=[smem, block3(rows), block3(rows)],
        out_specs=(
            block3(features),
            block3(2 * seen_rows),
            block3(features // 2),
        ),
        cost_estimate=cost(2 * buckets * rows * features**2, 2**22),
        compiler_params=pltpu.CompilerParams(vmem_limit_bytes=60 * 2**20),
        name="join_operators",
    )(core_flag, operators, operators_other)

    joined_block = block
    combiners = []
    eye = jnp.broadcast_to(jnp.eye(features, dtype=bf16), (buckets, features, features))
    prefix = eye
    prefixes = [eye]
    for s in range(stages - 1):
        far = [(i, i ^ (2 << s)) for i in range(segments)]
        rows_half = features // 2
        if s > 0:
            part = lax.dynamic_slice_in_dim(block, core * rows_half, rows_half, 1)
        if s == 0:
            scales = after(scales, part)
        part = lax.ppermute(part, "date", far)
        if s == 0:
            own = local(0, core_flag, scales)
            part = after(part, own)
        part_other = lax.ppermute(part, "date", swap)
        if s == 0:
            flags = jnp.concatenate([core_flag, ups[0]])
            straight, crossed = part, part_other
            if stages == 2:
                continue
        first = core == 0
        other = jnp.concatenate(
            [jnp.where(first, part, part_other), jnp.where(first, part_other, part)], axis=1
        )
        up = ups[s][0] == 1
        combiners.append(jnp.where(up, block, other))
        if s == 0:
            prefix = jnp.where(up, other, eye)
            prefixes.append(prefix)
        else:
            moved = jnp.einsum("bij,bjk->bik", prefix, other, preferred_element_type=f32)
            prefix = jnp.where(up, moved.astype(bf16), prefix)
            prefixes.append(prefix)
        if s < stages - 2:
            above = jnp.where(up, block, other)
            below = jnp.where(up, other, block)
            block = jnp.einsum(
                "bij,bjk->bik", above, below, preferred_element_type=f32
            ).astype(bf16)

    if stages < 2:
        own = local(0, core_flag, scales)

    ends = []
    seens = []
    table = []
    places = {}
    for b in range(buckets):
        unit = 0
        for size in chunks(pieces, b, buckets):
            for i in range(size * pair):
                places[b, unit * pair + i] = (len(table), i)
            table.append((b, unit, size))
            unit += size
    count = len(table)

    def join_states(b, own, late_half):
        sizes = [size for at, _, size in table if at == b]
        begin = 0
        for group in [sizes] if b == 0 else [sizes[:1], sizes[1:]]:
            units = sum(group)
            call = pl.pallas_call(
                functools.partial(join_state_kernel, b, begin, group),
                out_shape=(jax.ShapeDtypeStruct((units, 2 * seen_rows, width), bf16),)
                + tuple(jax.ShapeDtypeStruct((features, size * width), bf16) for size in group),
                in_specs=[smem] + [anywhere] * 4,
                out_specs=(vmem,) * (len(group) + 1),
                scratch_shapes=[
                    pltpu.VMEM((units, rows, width), bf16),
                    pltpu.VMEM((units, rows, width), bf16),
                    pltpu.VMEM((rows, features), bf16),
                    pltpu.SemaphoreType.DMA((units,)),
                    pltpu.SemaphoreType.DMA((units,)),
                    pltpu.SemaphoreType.DMA,
                ],
                compiler_params=small,
                cost_estimate=cost(2 * rows * features * units * width, 2**21),
                name="join_states",
            )
            result = call(core_flag, own, late_half, operators, operators_other)
            ends.extend(result[1:])
            unit = 0
            for size in group:
                seens.append((result[0], unit))
                unit += size
            begin += units

    weight_column = risk_weight[:, :, None]

    square = pltpu.VMEM((features, features), bf16)

    def first_stage(j, mine, other):
        return pl.pallas_call(
            functools.partial(first_stage_kernel, table[j][0]),
            out_shape=jax.ShapeDtypeStruct(mine.shape, bf16),
            in_specs=[smem, vmem, vmem] + [anywhere] * 3,
            out_specs=vmem,
            scratch_shapes=[square, pltpu.SemaphoreType.DMA((2,))],
            compiler_params=small,
            cost_estimate=cost(2 * features**2 * width, 2**20),
            name="stage",
        )(flags, mine, other, joined_block, straight, crossed)

    def stage(j, up, mine, other, combiner):
        return pl.pallas_call(
            functools.partial(stage_kernel, table[j][0]),
            out_shape=jax.ShapeDtypeStruct(mine.shape, bf16),
            in_specs=[smem, vmem, vmem, vmem],
            out_specs=vmem,
            compiler_params=small,
            cost_estimate=cost(2 * features**2 * width, 2**20),
            name="stage",
        )(up, mine, other, combiner)

    def final(j, up, first, last):
        b, _, size = table[j]
        halves = stages == 2
        prefix = (straight, crossed) if halves else (prefixes[-1],)
        flag = flags if halves else jnp.concatenate([core_flag, jnp.ones((1,), jnp.int32)])
        if not halves:
            first = jnp.where(up[0] == 1, first, jnp.zeros_like(first))
        return pl.pallas_call(
            functools.partial(final_kernel, b, seens[j][1], 2 * dates, halves),
            out_shape=jax.ShapeDtypeStruct((2, 2 * dates, size * width), f32),
            in_specs=[smem, vmem, vmem] + [anywhere] * (len(prefix) + 2) + [vmem] * 2,
            out_specs=vmem,
            scratch_shapes=[
                square,
                pltpu.VMEM((2 * seen_rows, features), bf16),
                pltpu.VMEM((size, 2 * seen_rows, width), bf16),
                pltpu.SemaphoreType.DMA((4,)),
            ],
            compiler_params=small,
            cost_estimate=cost(4 * features**2 * width, 2**21),
            name="final",
        )(flag, first, last, *prefix, seer, seens[j][0], weight_column, correlation)

    arrived = [[] for _ in range(stages)]
    leaving = [[] for _ in range(stages)]
    holds = {}
    results = []

    def held(s, j):
        if s == 0:
            return jnp.zeros(arrived[0][j].shape, bf16), jnp.ones((1,), jnp.int32)
        if s == 1:
            return arrived[0][j], ups[0]
        if (s, j) not in holds:
            before, flag = held(s - 1, j)
            before = jnp.where(flag[0] == 1, before, jnp.zeros_like(before)).astype(f32)
            moved = dot(prefixes[s - 1][table[j][0]], arrived[s - 1][j])
            value = jnp.where(ups[s - 1][0] == 1, before + moved, before)
            holds[s, j] = value.astype(bf16)
        return holds[s, j], jnp.ones((1,), jnp.int32)

    def advance(s, behind=None):
        j = len(arrived[s])
        last = s == stages - 1
        bit = 2 << s
        link = [(i, i ^ bit) for i in range(segments) if not (last and i & bit)]
        if s == 0:
            out = ends[j]
        else:
            near = arrived[s - 1][j]
            if behind is not None:
                near = after(near, results[behind])
            if s == 1:
                out = first_stage(j, leaving[0][j], near)
            else:
                out = stage(j, ups[s - 1], leaving[s - 1][j], near, combiners[s - 1])
        if j >= flight:
            out = after(out, arrived[s][j - flight])
        leaving[s].append(out)
        arrived[s].append(lax.ppermute(out, "date", link))

    def finish():
        i = len(results)
        if results:
            arrived[-1][i] = after(arrived[-1][i], results[-1])
        before, flag = held(stages - 1, i)
        results.append(final(i, flag, before, arrived[-1][i]))

    join_states(0, own, late_half)
    for b in range(buckets):
        for at, _, _ in table:
            if at == b:
                advance(0)
        if b + 1 < buckets:
            scales = after(scales, ends[-1])
            sent = local(b + 1, 1 - core_flag, scales)
            late_half = lax.ppermute(sent, "date", swap)
            scales = after(scales, sent)
            for _ in range(early if stages > 1 else 0):
                at = len(arrived[1])
                arrived[0][at] = after(arrived[0][at], sent)
                advance(1)
                scales = after(scales, leaving[1][-1])
            own = local(b + 1, core_flag, scales)
            join_states(b + 1, own, late_half)
    for s in range(1, stages):
        last = s == stages - 1
        if last:
            while len(arrived[s]) < 2:
                advance(s)
            discount, cross_gamma, step_days = lax.optimization_barrier(
                (discount, cross_gamma, step_days, leaving[s][-1])
            )[:3]
            discount = (step_days.astype(f32) / 365.0)[:, None, None] * discount
            discount_other = lax.ppermute(discount, "date", swap)
        while len(arrived[s]) < count:
            j = len(arrived[s])
            while last and len(results) < j - lag:
                finish()
            advance(s)
    while len(results) < count:
        finish()

    local_micro = discount.shape[1]
    both = jnp.where(
        core == 0,
        jnp.stack([discount, discount_other]),
        jnp.stack([discount_other, discount]),
    ).reshape(2 * dates, local_micro, lanes)
    high, low = split(jnp.swapaxes(both, 0, 1))
    carried = jnp.concatenate([high.reshape(-1, lanes), low.reshape(-1, lanes)], axis=0)
    body_rows = (buckets + 1) * half * 2 * dates
    message = pl.pallas_call(
        functools.partial(pack_kernel, places, buckets, half),
        out_shape=jax.ShapeDtypeStruct((body_rows + carried.shape[0], lanes), bf16),
        in_specs=[vmem] * (count + 1),
        out_specs=vmem,
        compiler_params=small,
        name="pack",
    )(*results, carried)
    gathered = [message]
    for k in range(1, zs):
        gathered.append(lax.ppermute(message, "bucket", [(i, (i + k) % zs) for i in range(zs)]))
    gamma = (
        0.5
        * (cross_gamma + cross_gamma.T)
        * (1.0 - jnp.eye(cross_gamma.shape[0], dtype=f32))
    )
    start = z * local_micro
    holder = start // half
    place = jnp.stack([z, core, start - holder * half]).astype(jnp.int32)
    out = pl.pallas_call(
        functools.partial(margin_kernel, buckets, 2 * dates, local_micro, half),
        out_shape=jax.ShapeDtypeStruct((local_micro + 1, 2 * dates, lanes), f32),
        in_specs=[smem] * 3 + [vmem] * zs,
        out_specs=vmem,
        scratch_shapes=[
            pltpu.VMEM((batches, 2 * dates, lanes), f32),
            pltpu.VMEM((half, 2 * dates, lanes), f32),
        ],
        compiler_params=small,
        name="margins",
    )(place, gamma, path_counts, *gathered)
    came = lax.ppermute(out, "date", swap)
    margin = jnp.where(holder == core, out[:local_micro], came[:local_micro])
    margin = lax.dynamic_slice_in_dim(margin, core * dates, dates, 1)
    margin = jnp.swapaxes(margin, 0, 1)
    total = out[local_micro] + came[local_micro]
    step = 2
    while step < segments:
        total = total + lax.ppermute(total, "date", [(i, i ^ step) for i in range(segments)])
        step *= 2
    return (margin, total[0, 0])


def solution(mesh):
    in_specs = (
        P("date", "bucket", None, None),
        P("date", "bucket", None, None, None),
        P("date"),
        P("bucket", None, None),
        P("bucket", None),
        P("bucket", None, None),
        P(),
        P("date", "bucket", None),
        P(),
    )
    out_specs = (P("date", "bucket", None), P())


    return jax.shard_map(shards, mesh=mesh, in_specs=in_specs, out_specs=out_specs, check_vma=False)
```
